512 devices in a mesh: depth: 8 (over x, core), harm: 64 (over z, y).
Axes of the slice: x: 4, y: 4, z: 16, core: 2. Of those that a mesh axis runs over, the one named last changes fastest.
Arguments:
- source: float32 [8, 8, 4096], P('depth', None, 'harm')
- coupling: bfloat16 [8, 4096, 4096], P('depth', 'harm'), may hold values from -0.125 to 0.125, as said below
- diagonal: float32 [8, 4096], P('depth', 'harm'), may hold values from 1.5 to 8
Outputs:
- solution: float32 [8, 8, 4096], P('depth', None, 'harm')
- residual: float32 [8, 8, 4096], P('depth', None, 'harm')
The draws below stay inside these ranges and needn't reach their ends.
Inputs may be any that keep to these rules, and one draw needn't show every extreme that they name: coupling[z] is symmetric for every plane z.
All inputs are finite; a program needn't handle non-finite values.
Results may differ from the reference program's by a relative error of at most 0.00083.
Values may be sent and summed in bfloat16 or wider, within the bound.
No kernel may reach another device: no remote copies, remote signals or barrier semaphores. Data moves between devices by JAX's collectives and lax.ppermute only.
A program may use at most 64 MiB of HBM per device.

```python
import math
import jax
import jax.numpy as jnp
from jax import lax

G = 4096
B = 8
ITERS = 2
Z = 8


def draw_coupling(key, part):
    plane_keys = jax.random.split(key, Z)

    def one_plane(plane_key):
        raw = jnp.clip(jax.random.normal(plane_key, (G, G), jnp.float32), -6.0, 6.0)
        return ((raw + raw.T) * (0.4 / math.sqrt(2.0 * G))).astype(jnp.bfloat16)
    return lax.map(one_plane, plane_keys)


def draw_source(key, part):
    harmonic = jnp.arange(G, dtype=jnp.float32) / G
    plane = jnp.arange(Z, dtype=jnp.float32) / Z
    profile = jnp.exp(0.5 * math.log(3.0) * (plane[:, None, None] + harmonic[None, None, :]))
    base = jnp.clip(jax.random.normal(key, (Z, B, G), jnp.float32), -6.0, 6.0)
    return base * profile


def block_scale(own_key, extent, cuts, smallest, largest):
    gain = 1.0
    for position, shards_of in cuts:
        heights = jax.random.uniform(jax.random.fold_in(jax.random.fold_in(own_key, 6), position), (shards_of,), jnp.float32, smallest / len(cuts), largest / len(cuts))
        gain = gain * jnp.repeat(jnp.exp(heights), extent[position] // shards_of).reshape((-1,) + (1,) * (len(extent) - 1 - position))
    return gain


def setup_inputs(seed: int = 0) -> dict:
    keys = jax.random.split(jax.random.key(seed), 4)
    return {
        "source": draw_source(jax.random.fold_in(keys[3], 71), 0),
        "coupling": draw_coupling(jax.random.fold_in(keys[3], 71), 0),
        "diagonal": jnp.clip(jnp.exp(math.log(8.0) - 1.6739764 * jax.random.uniform(keys[2], (Z, G), jnp.float32) ** block_scale(keys[2], (Z, G), ((0, 8), (1, 64)), -0.2, 0.2)), 1.5, 8.0),
    }


def plane_product(pair):
    return jnp.dot(pair[1], pair[0].T, preferred_element_type=jnp.float32)


def operate_on(vector_in, coupling, diagonal):
    narrow = vector_in.astype(jnp.bfloat16)
    blended = lax.map(plane_product, (coupling, narrow))
    padded = jnp.pad(vector_in, ((1, 1), (0, 0), (0, 0)))
    return (diagonal[:, None, :] + 2.0) * vector_in + blended - (padded[2:] + padded[:-2])


def inner_product(first, second):
    return jnp.sum(first * second, axis=(0, 2))


def reference(source, coupling, diagonal):
    solution = jnp.zeros_like(source)
    residual = source
    search = source
    rho_now = inner_product(source, residual)
    for iteration in range(ITERS):
        image_one = operate_on(search, coupling, diagonal)
        alpha_step = rho_now / inner_product(source, image_one)
        interim = residual - alpha_step[None, :, None] * image_one
        image_two = operate_on(interim, coupling, diagonal)
        omega_step = inner_product(image_two, interim) / inner_product(image_two, image_two)
        solution = solution + alpha_step[None, :, None] * search + omega_step[None, :, None] * interim
        residual = interim - omega_step[None, :, None] * image_two
        if iteration + 1 < ITERS:
            rho_next = inner_product(source, residual)
            beta_step = (rho_next / rho_now) * (alpha_step / omega_step)
            search = residual + beta_step[None, :, None] * (search - omega_step[None, :, None] * image_one)
            rho_now = rho_next
    return solution, residual
```

```python
import jax
import jax.numpy as jnp
from jax import lax
from jax.experimental import pallas as pl
from jax.experimental.pallas import tpu as pltpu
from jax.sharding import Mesh, PartitionSpec as P

STEPS = 4
CENTRE = 6.75
SCALE = 32.0
PAIRS = [(i, j) for j in range(STEPS + 1) for i in range(j + 1)]
NZ, NY, NX, NC = 16, 4, 4, 2
B = 8
H = 64
W = NY * H
F32 = jnp.float32
BF16 = jnp.bfloat16


def call(body, outs, *args, smem=0):
    specs = [pl.BlockSpec(memory_space=pltpu.SMEM)] * smem
    specs += [pl.BlockSpec(memory_space=pltpu.VMEM)] * (len(args) - smem)
    return pl.pallas_call(
        body,
        out_shape=outs,
        in_specs=specs,
        out_specs=jax.tree.map(lambda _: pl.BlockSpec(memory_space=pltpu.VMEM), outs),
    )(*args)


def store_parts(send, field, row):
    turned = pltpu.roll(field, row * H, 1)
    high = turned.astype(BF16)
    low = (turned - high.astype(F32)).astype(BF16)
    both = jnp.concatenate([high, low], axis=0)
    for z in range(NZ):
        send[z] = both


def unpack(row_ref, packed, field_out, diag_out, send):
    row = row_ref[0]
    field = jnp.concatenate([packed[y][:, :H] for y in range(NY)], axis=1)
    diag = jnp.concatenate([packed[y][:, H:] for y in range(NY)], axis=1)
    both = jnp.concatenate([field, diag], axis=0)
    both = pltpu.roll(both, (NY - row) % NY * H, 1)
    field_out[...] = both[:B]
    diag_out[...] = both[B:]
    store_parts(send, both[:B], row)


def next_field(parts, blocks, field, diag, up, down):
    sums = []
    for block in blocks:
        total = None
        for z in range(NZ):
            term = lax.dot_general(
                parts[z],
                block[:, z * W : (z + 1) * W],
                (((1,), (1,)), ((), ())),
                preferred_element_type=F32,
            )
            total = term if total is None else total + term
        sums.append(total[:B] + total[B:])
    blended = jnp.concatenate(sums, axis=1)
    own = (diag[0:1] + (2.0 - CENTRE)) * field[...]
    return (own + blended - (up[...] + down[...])) * (1.0 / SCALE)


def step(row_ref, parts, c0, c1, c2, c3, field, diag, up, down, field_out, send):
    out = next_field(parts, (c0, c1, c2, c3), field, diag, up, down)
    field_out[...] = out
    store_parts(send, out, row_ref[0])


def last_step(parts, c0, c1, c2, c3, field, diag, up, down, f0, f1, f2, field_out, send):
    out = next_field(parts, (c0, c1, c2, c3), field, diag, up, down)
    field_out[...] = out[:, :H]
    fields = [f0[...], f1[...], f2[...], field[...], out]
    lane = lax.broadcasted_iota(jnp.int32, (B, 128), 1)
    table = jnp.zeros((B, 128), F32)
    for p, (i, j) in enumerate(PAIRS):
        table = jnp.where(lane == p, jnp.sum(fields[i] * fields[j], axis=1, keepdims=True), table)
    for k in range(NX * NC):
        send[k] = table


def add_up(tables, send):
    total = tables[0]
    for k in range(1, NX * NC):
        total = total + tables[k]
    for z in range(NZ):
        send[z] = total


def finish(tables, f0, f1, f2, f3, f4, solution_out, residual_out):
    total = tables[0]
    for z in range(1, NZ):
        total = total + tables[z]
    gram = {}
    for p, (i, j) in enumerate(PAIRS):
        gram[i, j] = gram[j, i] = total[:, p : p + 1]

    def inner(a, c):
        total = None
        for j, cj in enumerate(c):
            part = None
            for i, ai in enumerate(a):
                term = gram[i, j] if ai is None else ai * gram[i, j]
                part = term if part is None else part + term
            part = part if cj is None else part * cj
            total = part if total is None else total + part
        return total

    def plus(a, c, scale):
        out = []
        for k in range(max(len(a), len(c))):
            if k >= len(c):
                out.append(a[k])
            elif k >= len(a):
                out.append(scale * c[k])
            else:
                out.append(a[k] + scale * c[k])
        return out

    def image(a):
        out = [CENTRE * x for x in a] + [jnp.zeros_like(a[0])]
        for k, x in enumerate(a):
            out[k + 1] = out[k + 1] + SCALE * x
        return out

    one = jnp.ones((B, 1), F32)
    source = [None]
    found = None
    residual = search = [one]
    rho = gram[0, 0]
    for iteration in range(2):
        image_one = image(search)
        alpha = rho / inner(source, image_one)
        interim = plus(residual, image_one, -alpha)
        image_two = image(interim)
        omega = inner(image_two, interim) / inner(image_two, image_two)
        if found is None:
            found = [alpha * x for x in search]
        else:
            found = plus(found, search, alpha)
        found = plus(found, interim, omega)
        residual = plus(interim, image_two, -omega)
        if iteration == 0:
            rho_next = inner(source, residual)
            beta = (rho_next / rho) * (alpha / omega)
            search = plus(residual, plus(search, image_one, -omega), beta)
            rho = rho_next
    fields = [f0[:, :H], f1[:, :H], f2[:, :H], f3[:, :H], f4[...]]

    def combine(a):
        out = a[0] * fields[0]
        for k in range(1, len(a)):
            out = out + a[k] * fields[k]
        return out

    solution_out[...] = combine(found)
    residual_out[...] = combine(residual)


def spread(array, axes, count):
    return lax.all_to_all(array, axes, 0, 0, tiled=True)


def neighbours(field):
    ends = NX * NC - 1
    up = lax.ppermute(field, ("x", "c"), [(i, i + 1) for i in range(ends)])
    down = lax.ppermute(field, ("x", "c"), [(i + 1, i) for i in range(ends)])
    return up, down


def on_device(source, coupling, diagonal):
    own = coupling[0]
    row = lax.axis_index("y").astype(jnp.int32).reshape(1)
    blocks = [own]
    for shift in range(1, NY):
        blocks.append(lax.ppermute(own, "y", [((y + shift) % NY, y) for y in range(NY)]))
    packed = jnp.concatenate([source[0], jnp.broadcast_to(diagonal, (B, H))], axis=1)
    packed = lax.all_to_all(jnp.broadcast_to(packed[None], (NY, B, 128)), "y", 0, 0, tiled=True)
    shape = jax.ShapeDtypeStruct
    field_shape, send_shape = shape((B, W), F32), shape((NZ, 2 * B, W), BF16)
    field, diag, send = call(unpack, (field_shape, field_shape, send_shape), row, packed, smem=1)
    fields = [field]
    for k in range(STEPS):
        up, down = neighbours(field)
        parts = lax.all_to_all(send, "z", 0, 0, tiled=True)
        if k + 1 < STEPS:
            field, send = call(
                step, (field_shape, send_shape), row, parts, *blocks, field, diag, up, down, smem=1
            )
            fields.append(field)
        else:
            last, table = call(
                last_step,
                (shape((B, H), F32), shape((NX * NC, B, 128), F32)),
                parts, *blocks, field, diag, up, down, *fields[:3],
            )
    table = lax.all_to_all(table, ("x", "c"), 0, 0, tiled=True)
    table = call(add_up, shape((NZ, B, 128), F32), table)
    table = lax.all_to_all(table, "z", 0, 0, tiled=True)
    own_shape = shape((B, H), F32)
    found, residual = call(finish, (own_shape, own_shape), table, *fields, last)
    return found[None], residual[None]


def solution(mesh):
    fine = Mesh(mesh.devices.reshape(NX, NC, NZ, NY), ("x", "c", "z", "y"))
    depth, harm = ("x", "c"), ("z", "y")
    return jax.shard_map(
        on_device,
        mesh=fine,
        in_specs=(P(depth, None, harm), P(depth, harm, None), P(depth, harm)),
        out_specs=(P(depth, None, harm), P(depth, None, harm)),
        check_vma=False,
    )
```

```python
import jax
import jax.numpy as jnp
from jax import lax
from jax.experimental import pallas as pl
from jax.experimental.pallas import tpu as pltpu
from jax.sharding import Mesh, PartitionSpec as P

STEPS = 4
CENTRE = 6.75
SCALE = 32.0
PAIRS = [(i, j) for j in range(STEPS + 1) for i in range(j + 1)]
NZ, NY, NX, NC = 16, 4, 4, 2
B = 8
H = 64
W = NY * H
F32 = jnp.float32
BF16 = jnp.bfloat16


def call(body, outs, *args, smem=0):
    args = args[:smem] + tuple(
        pltpu.with_memory_space_constraint(x, pltpu.VMEM) for x in args[smem:]
    )
    outs = jax.tree.map(lambda o: pltpu.VMEM(o.shape, o.dtype), outs)
    specs = [pl.BlockSpec(memory_space=pltpu.SMEM)] * smem
    specs += [pl.BlockSpec(memory_space=pltpu.VMEM)] * (len(args) - smem)
    return pl.pallas_call(
        body,
        out_shape=outs,
        in_specs=specs,
        out_specs=jax.tree.map(lambda _: pl.BlockSpec(memory_space=pltpu.VMEM), outs),
    )(*args)


def store_parts(send, field, row):
    turned = pltpu.roll(field, row * H, 1)
    high = turned.astype(BF16)
    low = (turned - high.astype(F32)).astype(BF16)
    both = jnp.concatenate([high, low], axis=0)
    for z in range(NZ):
        send[z] = both


def unpack(row_ref, packed, field_out, diag_out, send):
    row = row_ref[0]
    field = jnp.concatenate([packed[y][:, :H] for y in range(NY)], axis=1)
    diag = jnp.concatenate([packed[y][:, H:] for y in range(NY)], axis=1)
    both = jnp.concatenate([field, diag], axis=0)
    both = pltpu.roll(both, (NY - row) % NY * H, 1)
    field_out[...] = both[:B]
    diag_out[...] = both[B:]
    store_parts(send, both[:B], row)


def next_field(parts, blocks, field, diag, up, down):
    sums = []
    for block in blocks:
        total = None
        for z in range(NZ):
            term = lax.dot_general(
                parts[z],
                block[:, z * W : (z + 1) * W],
                (((1,), (1,)), ((), ())),
                preferred_element_type=F32,
            )
            total = term if total is None else total + term
        sums.append(total[:B] + total[B:])
    blended = jnp.concatenate(sums, axis=1)
    own = (diag[0:1] + (2.0 - CENTRE)) * field[...]
    return (own + blended - (up[...] + down[...])) * (1.0 / SCALE)


def step(row_ref, parts, c0, c1, c2, c3, c4, field, diag, up, down, field_out, send):
    out = next_field(parts, (c0, c1, c2, c3, c4), field, diag, up, down)
    field_out[...] = out
    store_parts(send, out, row_ref[0])


def last_step(parts, c0, c1, c2, c3, c4, field, diag, up, down, f0, f1, f2, field_out, send):
    out = next_field(parts, (c0, c1, c2, c3, c4), field, diag, up, down)
    field_out[...] = out[:, :H]
    fields = [f0[...], f1[...], f2[...], field[...], out]
    lane = lax.broadcasted_iota(jnp.int32, (B, 128), 1)
    table = jnp.zeros((B, 128), F32)
    for p, (i, j) in enumerate(PAIRS):
        table = jnp.where(lane == p, jnp.sum(fields[i] * fields[j], axis=1, keepdims=True), table)
    for k in range(NX * NC):
        send[k] = table


def add_up(tables, send):
    total = tables[0]
    for k in range(1, NX * NC):
        total = total + tables[k]
    for z in range(NZ):
        send[z] = total


def finish(tables, f0, f1, f2, f3, f4, solution_out, residual_out):
    total = tables[0]
    for z in range(1, NZ):
        total = total + tables[z]
    gram = {}
    for p, (i, j) in enumerate(PAIRS):
        gram[i, j] = gram[j, i] = total[:, p : p + 1]

    def inner(a, c):
        total = None
        for j, cj in enumerate(c):
            part = None
            for i, ai in enumerate(a):
                term = gram[i, j] if ai is None else ai * gram[i, j]
                part = term if part is None else part + term
            part = part if cj is None else part * cj
            total = part if total is None else total + part
        return total

    def plus(a, c, scale):
        out = []
        for k in range(max(len(a), len(c))):
            if k >= len(c):
                out.append(a[k])
            elif k >= len(a):
                out.append(scale * c[k])
            else:
                out.append(a[k] + scale * c[k])
        return out

    def image(a):
        out = [CENTRE * x for x in a] + [jnp.zeros_like(a[0])]
        for k, x in enumerate(a):
            out[k + 1] = out[k + 1] + SCALE * x
        return out

    one = jnp.ones((B, 1), F32)
    source = [None]
    found = None
    residual = search = [one]
    rho = gram[0, 0]
    for iteration in range(2):
        image_one = image(search)
        alpha = rho / inner(source, image_one)
        interim = plus(residual, image_one, -alpha)
        image_two = image(interim)
        omega = inner(image_two, interim) / inner(image_two, image_two)
        if found is None:
            found = [alpha * x for x in search]
        else:
            found = plus(found, search, alpha)
        found = plus(found, interim, omega)
        residual = plus(interim, image_two, -omega)
        if iteration == 0:
            rho_next = inner(source, residual)
            beta = (rho_next / rho) * (alpha / omega)
            search = plus(residual, plus(search, image_one, -omega), beta)
            rho = rho_next
    fields = [f0[:, :H], f1[:, :H], f2[:, :H], f3[:, :H], f4[...]]

    def combine(a):
        out = a[0] * fields[0]
        for k in range(1, len(a)):
            out = out + a[k] * fields[k]
        return out

    solution_out[...] = combine(found)
    residual_out[...] = combine(residual)


def spread(array, axes, count):
    return lax.all_to_all(array, axes, 0, 0, tiled=True)


def shifted(array, shift):
    return lax.ppermute(array, "y", [((y + shift) % NY, y) for y in range(NY)])


def neighbours(field):
    ends = NX * NC - 1
    up = lax.ppermute(field, ("x", "c"), [(i, i + 1) for i in range(ends)])
    down = lax.ppermute(field, ("x", "c"), [(i + 1, i) for i in range(ends)])
    return up, down


def on_device(source, coupling, diagonal):
    own = coupling[0]
    row = lax.axis_index("y").astype(jnp.int32).reshape(1)
    packed = jnp.concatenate([source[0], jnp.broadcast_to(diagonal, (B, H))], axis=1)
    packed = lax.all_to_all(jnp.broadcast_to(packed[None], (NY, B, 128)), "y", 0, 0, tiled=True)
    own, packed = lax.optimization_barrier((own, packed))
    after, before = shifted(own, 1), shifted(own, -1)
    blocks = [own, after, shifted(after[: H // 2], 1), shifted(before[H // 2 :], -1), before]
    shape = jax.ShapeDtypeStruct
    field_shape, send_shape = shape((B, W), F32), shape((NZ, 2 * B, W), BF16)
    field, diag, send = call(unpack, (field_shape, field_shape, send_shape), row, packed, smem=1)
    fields = [field]
    for k in range(STEPS):
        up, down = neighbours(field)
        parts = lax.all_to_all(send, "z", 0, 0, tiled=True)
        if k + 1 < STEPS:
            field, send = call(
                step, (field_shape, send_shape), row, parts, *blocks, field, diag, up, down, smem=1
            )
            fields.append(field)
        else:
            last, table = call(
                last_step,
                (shape((B, H), F32), shape((NX * NC, B, 128), F32)),
                parts, *blocks, field, diag, up, down, *fields[:3],
            )
    table = lax.all_to_all(table, ("x", "c"), 0, 0, tiled=True)
    table = call(add_up, shape((NZ, B, 128), F32), table)
    table = lax.all_to_all(table, "z", 0, 0, tiled=True)
    own_shape = shape((B, H), F32)
    found, residual = call(finish, (own_shape, own_shape), table, *fields, last)
    return found[None], residual[None]


def solution(mesh):
    fine = Mesh(mesh.devices.reshape(NX, NC, NZ, NY), ("x", "c", "z", "y"))
    depth, harm = ("x", "c"), ("z", "y")
    return jax.shard_map(
        on_device,
        mesh=fine,
        in_specs=(P(depth, None, harm), P(depth, harm, None), P(depth, harm)),
        out_specs=(P(depth, None, harm), P(depth, None, harm)),
        check_vma=False,
    )
```

```python
import jax
import jax.numpy as jnp
from jax import lax
from jax.experimental import pallas as pl
from jax.experimental.pallas import tpu as pltpu
from jax.sharding import Mesh, PartitionSpec as P

STEPS = 4
LOW_FROM = 2
CENTRE = 6.75
SCALE = 32.0
PAIRS = [(i, j) for j in range(STEPS + 1) for i in range(j + 1)]
NZ, NY, NX, NC = 16, 4, 4, 2
B = 8
H = 64
W = NY * H
F32 = jnp.float32
BF16 = jnp.bfloat16


def call(body, outs, *args, smem=0, keep=True):
    args = args[:smem] + tuple(
        pltpu.with_memory_space_constraint(x, pltpu.VMEM) for x in args[smem:]
    )
    if keep:
        outs = jax.tree.map(lambda o: pltpu.VMEM(o.shape, o.dtype), outs)
    specs = [pl.BlockSpec(memory_space=pltpu.SMEM)] * smem
    specs += [pl.BlockSpec(memory_space=pltpu.VMEM)] * (len(args) - smem)
    return pl.pallas_call(
        body,
        out_shape=outs,
        in_specs=specs,
        out_specs=jax.tree.map(lambda _: pl.BlockSpec(memory_space=pltpu.VMEM), outs),
    )(*args)


def store_parts(send, field, row):
    turned = pltpu.roll(field, row * H, 1)
    parts = turned.astype(BF16)
    if send.shape[1] > B:
        low = (turned - parts.astype(F32)).astype(BF16)
        parts = jnp.concatenate([parts, low], axis=0)
    for z in range(NZ):
        send[z] = parts


def unpack(row_ref, packed, field_out, diag_out, send):
    row = row_ref[0]
    field = jnp.concatenate([packed[y][:, :H] for y in range(NY)], axis=1)
    diag = jnp.concatenate([packed[y][:, H:] for y in range(NY)], axis=1)
    both = jnp.concatenate([field, diag], axis=0)
    both = pltpu.roll(both, (NY - row) % NY * H, 1)
    field_out[...] = both[:B]
    diag_out[...] = both[B:]
    store_parts(send, both[:B], row)


def next_field(parts, blocks, field, diag, up, down):
    sums = []
    for block in blocks:
        total = None
        for z in range(NZ):
            term = lax.dot_general(
                parts[z],
                block[:, z * W : (z + 1) * W],
                (((1,), (1,)), ((), ())),
                preferred_element_type=F32,
            )
            total = term if total is None else total + term
        sums.append(total if total.shape[0] == B else total[:B] + total[B:])
    blended = jnp.concatenate(sums, axis=1)
    own = (diag[0:1] + (2.0 - CENTRE)) * field[...]
    return (own + blended - (up[...] + down[...])) * (1.0 / SCALE)


def step(row_ref, parts, c0, c1, c2, c3, field, diag, up, down, field_out, send):
    out = next_field(parts, (c0, c1, c2, c3), field, diag, up, down)
    field_out[...] = out
    store_parts(send, out, row_ref[0])


def last_step(parts, c0, c1, c2, c3, field, diag, up, down, f0, f1, f2, field_out, send):
    out = next_field(parts, (c0, c1, c2, c3), field, diag, up, down)
    field_out[...] = out[:, :H]
    fields = [f0[...], f1[...], f2[...], field[...], out]
    lane = lax.broadcasted_iota(jnp.int32, (B, 128), 1)
    table = jnp.zeros((B, 128), F32)
    for p, (i, j) in enumerate(PAIRS):
        table = jnp.where(lane == p, jnp.sum(fields[i] * fields[j], axis=1, keepdims=True), table)
    for k in range(NX * NC):
        send[k] = table


def add_up(tables, send):
    total = tables[0]
    for k in range(1, NX * NC):
        total = total + tables[k]
    for z in range(NZ):
        send[z] = total


def finish(tables, f0, f1, f2, f3, f4, solution_out, residual_out):
    total = tables[0]
    for z in range(1, NZ):
        total = total + tables[z]
    gram = {}
    for p, (i, j) in enumerate(PAIRS):
        gram[i, j] = gram[j, i] = total[:, p : p + 1]

    def inner(a, c):
        total = None
        for j, cj in enumerate(c):
            part = None
            for i, ai in enumerate(a):
                term = gram[i, j] if ai is None else ai * gram[i, j]
                part = term if part is None else part + term
            part = part if cj is None else part * cj
            total = part if total is None else total + part
        return total

    def plus(a, c, scale):
        out = []
        for k in range(max(len(a), len(c))):
            if k >= len(c):
                out.append(a[k])
            elif k >= len(a):
                out.append(scale * c[k])
            else:
                out.append(a[k] + scale * c[k])
        return out

    def image(a):
        out = [CENTRE * x for x in a] + [jnp.zeros_like(a[0])]
        for k, x in enumerate(a):
            out[k + 1] = out[k + 1] + SCALE * x
        return out

    one = jnp.ones((B, 1), F32)
    source = [None]
    found = None
    residual = search = [one]
    rho = gram[0, 0]
    for iteration in range(2):
        image_one = image(search)
        alpha = rho / inner(source, image_one)
        interim = plus(residual, image_one, -alpha)
        image_two = image(interim)
        omega = inner(image_two, interim) / inner(image_two, image_two)
        if found is None:
            found = [alpha * x for x in search]
        else:
            found = plus(found, search, alpha)
        found = plus(found, interim, omega)
        residual = plus(interim, image_two, -omega)
        if iteration == 0:
            rho_next = inner(source, residual)
            beta = (rho_next / rho) * (alpha / omega)
            search = plus(residual, plus(search, image_one, -omega), beta)
            rho = rho_next
    fields = [f0[:, :H], f1[:, :H], f2[:, :H], f3[:, :H], f4[...]]

    def combine(a):
        out = a[0] * fields[0]
        for k in range(1, len(a)):
            out = out + a[k] * fields[k]
        return out

    solution_out[...] = combine(found)
    residual_out[...] = combine(residual)


def spread(array, axes, count):
    return lax.all_to_all(array, axes, 0, 0, tiled=True)


def shifted(array, shift):
    return lax.ppermute(array, "y", [((y + shift) % NY, y) for y in range(NY)])


def neighbours(field):
    count = NX * NC
    even = lax.ppermute(field, ("x", "c"), [(i, i ^ 1) for i in range(count)])
    pairs = [(i, i + 1) for i in range(1, count - 1, 2)]
    odd = lax.ppermute(field, ("x", "c"), pairs + [(j, i) for i, j in pairs])
    return even, odd


def on_device(source, coupling, diagonal):
    own = coupling[0]
    row = lax.axis_index("y").astype(jnp.int32).reshape(1)
    packed = jnp.concatenate([source[0], jnp.broadcast_to(diagonal, (B, H))], axis=1)
    packed = lax.all_to_all(jnp.broadcast_to(packed[None], (NY, B, 128)), "y", 0, 0, tiled=True)
    own, packed = lax.optimization_barrier((own, packed))
    blocks = [own] + [shifted(own, shift) for shift in range(1, NY)]
    shape = jax.ShapeDtypeStruct
    field_shape = shape((B, W), F32)
    send_shapes = [shape((NZ, B if k < LOW_FROM else 2 * B, W), BF16) for k in range(STEPS)]
    field, diag, send = call(unpack, (field_shape, field_shape, send_shapes[0]), row, packed, smem=1)
    fields = [field]
    for k in range(STEPS):
        up, down = neighbours(field)
        parts = lax.all_to_all(send, "z", 0, 0, tiled=True)
        if k + 1 < STEPS:
            field, send = call(
                step, (field_shape, send_shapes[k + 1]), row, parts, *blocks, field, diag, up, down, smem=1
            )
            fields.append(field)
        else:
            last, table = call(
                last_step,
                (shape((B, H), F32), shape((NX * NC, B, 128), F32)),
                parts, *blocks, field, diag, up, down, *fields[:3],
            )
    table = lax.all_to_all(table, ("x", "c"), 0, 0, tiled=True)
    table = call(add_up, shape((NZ, B, 128), F32), table)
    table = lax.all_to_all(table, "z", 0, 0, tiled=True)
    own_shape = shape((B, H), F32)
    found, residual = call(finish, (own_shape, own_shape), table, *fields, last, keep=False)
    return found[None], residual[None]


def solution(mesh):
    fine = Mesh(mesh.devices.reshape(NX, NC, NZ, NY), ("x", "c", "z", "y"))
    depth, harm = ("x", "c"), ("z", "y")
    return jax.shard_map(
        on_device,
        mesh=fine,
        in_specs=(P(depth, None, harm), P(depth, harm, None), P(depth, harm)),
        out_specs=(P(depth, None, harm), P(depth, None, harm)),
        check_vma=False,
    )
```

```python
import jax
import jax.numpy as jnp
from jax import lax
from jax.experimental import pallas as pl
from jax.experimental.pallas import tpu as pltpu
from jax.sharding import Mesh, PartitionSpec as P

STEPS = 4
LOW_FROM = 2
CENTRE = 6.75
SCALE = 32.0
PAIRS = [(i, j) for j in range(STEPS + 1) for i in range(j + 1)]
NZ, NY, NX, NC = 16, 4, 4, 2
B = 8
H = 64
W = NY * H
F32 = jnp.float32
BF16 = jnp.bfloat16


def call(body, outs, *args, smem=0, keep=True):
    args = args[:smem] + tuple(
        pltpu.with_memory_space_constraint(x, pltpu.VMEM) for x in args[smem:]
    )
    if keep:
        outs = jax.tree.map(lambda o: pltpu.VMEM(o.shape, o.dtype), outs)
    specs = [pl.BlockSpec(memory_space=pltpu.SMEM)] * smem
    specs += [pl.BlockSpec(memory_space=pltpu.VMEM)] * (len(args) - smem)
    return pl.pallas_call(
        body,
        out_shape=outs,
        in_specs=specs,
        compiler_params=pltpu.CompilerParams(vmem_limit_bytes=8 << 20),
        out_specs=jax.tree.map(lambda _: pl.BlockSpec(memory_space=pltpu.VMEM), outs),
    )(*args)


def store_parts(send, field, row):
    turned = pltpu.roll(field, row * H, 1)
    parts = turned.astype(BF16)
    if send.shape[1] > B:
        low = (turned - parts.astype(F32)).astype(BF16)
        parts = jnp.concatenate([parts, low], axis=0)
    for z in range(NZ):
        send[z] = parts


def unpack(row_ref, packed, field_out, even_out, diag_out, send):
    row = row_ref[0] % NY
    core = row_ref[0] // NY

    def wide(which, columns):
        joined = jnp.concatenate([packed[which * NY + y][:, columns] for y in range(NY)], axis=1)
        return pltpu.roll(joined, (NY - row) % NY * H, 1)

    field = wide(core, slice(0, H))
    field_out[...] = field
    even_out[...] = wide(1 - core, slice(0, H))
    diag_out[...] = wide(core, slice(H, 2 * H))
    store_parts(send, field, row)


def next_field(parts, blocks, field, diag, up, down):
    sums = []
    for block in blocks:
        total = None
        for z in range(NZ):
            term = lax.dot_general(
                parts[z],
                block[:, z * W : (z + 1) * W],
                (((1,), (1,)), ((), ())),
                preferred_element_type=F32,
            )
            total = term if total is None else total + term
        sums.append(total if total.shape[0] == B else total[:B] + total[B:])
    blended = jnp.concatenate(sums, axis=1)
    own = (diag[0:1] + (2.0 - CENTRE)) * field[...]
    return (own + blended - (up[...] + down[...])) * (1.0 / SCALE)


def step(row_ref, parts, c0, c1, c2, c3, field, diag, up, down, field_out, send):
    out = next_field(parts, (c0, c1, c2, c3), field, diag, up, down)
    field_out[...] = out
    store_parts(send, out, row_ref[0] % NY)


def last_step(parts, c0, c1, c2, c3, field, diag, up, down, f0, f1, f2, field_out, send):
    out = next_field(parts, (c0, c1, c2, c3), field, diag, up, down)
    field_out[...] = out[:, :H]
    fields = [f0[...], f1[...], f2[...], field[...], out]
    lane = lax.broadcasted_iota(jnp.int32, (B, 128), 1)
    table = jnp.zeros((B, 128), F32)
    for p, (i, j) in enumerate(PAIRS):
        table = jnp.where(lane == p, jnp.sum(fields[i] * fields[j], axis=1, keepdims=True), table)
    for k in range(NX * NC):
        send[k] = table


def add_up(tables, send):
    total = tables[0]
    for k in range(1, NX * NC):
        total = total + tables[k]
    for z in range(NZ):
        send[z] = total


def finish(tables, f0, f1, f2, f3, f4, solution_out, residual_out):
    total = tables[0]
    for z in range(1, NZ):
        total = total + tables[z]
    gram = {}
    for p, (i, j) in enumerate(PAIRS):
        gram[i, j] = gram[j, i] = total[:, p : p + 1]

    def inner(a, c):
        total = None
        for j, cj in enumerate(c):
            part = None
            for i, ai in enumerate(a):
                term = gram[i, j] if ai is None else ai * gram[i, j]
                part = term if part is None else part + term
            part = part if cj is None else part * cj
            total = part if total is None else total + part
        return total

    def plus(a, c, scale):
        out = []
        for k in range(max(len(a), len(c))):
            if k >= len(c):
                out.append(a[k])
            elif k >= len(a):
                out.append(scale * c[k])
            else:
                out.append(a[k] + scale * c[k])
        return out

    def image(a):
        out = [CENTRE * x for x in a] + [jnp.zeros_like(a[0])]
        for k, x in enumerate(a):
            out[k + 1] = out[k + 1] + SCALE * x
        return out

    one = jnp.ones((B, 1), F32)
    source = [None]
    found = None
    residual = search = [one]
    rho = gram[0, 0]
    for iteration in range(2):
        image_one = image(search)
        alpha = rho / inner(source, image_one)
        interim = plus(residual, image_one, -alpha)
        image_two = image(interim)
        omega = inner(image_two, interim) / inner(image_two, image_two)
        if found is None:
            found = [alpha * x for x in search]
        else:
            found = plus(found, search, alpha)
        found = plus(found, interim, omega)
        residual = plus(interim, image_two, -omega)
        if iteration == 0:
            rho_next = inner(source, residual)
            beta = (rho_next / rho) * (alpha / omega)
            search = plus(residual, plus(search, image_one, -omega), beta)
            rho = rho_next
    fields = [f0[:, :H], f1[:, :H], f2[:, :H], f3[:, :H], f4[...]]

    def combine(a):
        out = a[0] * fields[0]
        for k in range(1, len(a)):
            out = out + a[k] * fields[k]
        return out

    solution_out[...] = combine(found)
    residual_out[...] = combine(residual)


def spread(array, axes, count):
    return lax.all_to_all(array, axes, 0, 0, tiled=True)


def shifted(array, shift):
    return lax.ppermute(array, "y", [((y + shift) % NY, y) for y in range(NY)])


def even(field):
    return lax.ppermute(field, ("x", "c"), [(i, i ^ 1) for i in range(NX * NC)])


def odd(field):
    pairs = [(i, i + 1) for i in range(1, NX * NC - 1, 2)]
    return lax.ppermute(field, ("x", "c"), pairs + [(j, i) for i, j in pairs])


def on_device(source, coupling, diagonal):
    own = coupling[0]
    row = lax.axis_index(("c", "y")).astype(jnp.int32).reshape(1)
    packed = jnp.concatenate([source[0], jnp.broadcast_to(diagonal, (B, H))], axis=1)
    packed = jnp.broadcast_to(packed[None], (NC * NY, B, 128))
    packed = lax.all_to_all(packed, ("c", "y"), 0, 0, tiled=True)
    own, packed = lax.optimization_barrier((own, packed))
    blocks = [own] + [shifted(own, shift) for shift in range(1, NY)]
    shape = jax.ShapeDtypeStruct
    wide = shape((B, W), F32)
    sends = [shape((NZ, B if k < LOW_FROM else 2 * B, W), BF16) for k in range(STEPS)]
    field, up, diag, send = call(unpack, (wide, wide, wide, sends[0]), row, packed, smem=1)
    fields = [field]
    for k in range(STEPS):
        down = odd(field)
        if k > 0:
            up = even(field)
        parts = lax.all_to_all(send, "z", 0, 0, tiled=True)
        if k + 1 < STEPS:
            field, send = call(
                step,
                (wide, sends[k + 1]),
                row, parts, *blocks, field, diag, up, down,
                smem=1,

            )
            fields.append(field)
        else:
            last, table = call(
                last_step,
                (shape((B, H), F32), shape((NX * NC, B, 128), F32)),
                parts, *blocks, field, diag, up, down, *fields[:3],
            )
    table = lax.all_to_all(table, ("x", "c"), 0, 0, tiled=True)
    table = call(add_up, shape((NZ, B, 128), F32), table)
    table = lax.all_to_all(table, "z", 0, 0, tiled=True)
    own_shape = shape((B, H), F32)
    found, residual = call(finish, (own_shape, own_shape), table, *fields, last, keep=False)
    return found[None], residual[None]


def solution(mesh):
    fine = Mesh(mesh.devices.reshape(NX, NC, NZ, NY), ("x", "c", "z", "y"))
    depth, harm = ("x", "c"), ("z", "y")
    return jax.shard_map(
        on_device,
        mesh=fine,
        in_specs=(P(depth, None, harm), P(depth, harm, None), P(depth, harm)),
        out_specs=(P(depth, None, harm), P(depth, None, harm)),
        check_vma=False,
    )
```

```python
import jax
import jax.numpy as jnp
from jax import lax
from jax.experimental import pallas as pl
from jax.experimental.pallas import tpu as pltpu
from jax.sharding import Mesh, PartitionSpec as P

STEPS = 4
LOW_FROM = 2
CENTRE = 6.75
SCALE = 32.0
PAIRS = [(i, j) for j in range(STEPS + 1) for i in range(j + 1)]
NZ, NY, NX, NC = 16, 4, 4, 2
B = 8
H = 64
W = NY * H
F32 = jnp.float32
BF16 = jnp.bfloat16


def call(body, outs, *args, smem=0, loose=(), keep=True):
    args = args[:smem] + tuple(
        x if i in loose else pltpu.with_memory_space_constraint(x, pltpu.VMEM)
        for i, x in enumerate(args[smem:])
    )
    if keep:
        outs = jax.tree.map(lambda o: pltpu.VMEM(o.shape, o.dtype), outs)
    specs = [pl.BlockSpec(memory_space=pltpu.SMEM)] * smem
    specs += [pl.BlockSpec(memory_space=pltpu.VMEM)] * (len(args) - smem)
    return pl.pallas_call(
        body,
        out_shape=outs,
        in_specs=specs,
        compiler_params=pltpu.CompilerParams(vmem_limit_bytes=8 << 20),
        out_specs=jax.tree.map(lambda _: pl.BlockSpec(memory_space=pltpu.VMEM), outs),
    )(*args)


def store_parts(send, field):
    parts = field.astype(BF16)
    if send.shape[1] > B:
        low = (field - parts.astype(F32)).astype(BF16)
        parts = jnp.concatenate([parts, low], axis=0)
    for z in range(NZ):
        send[z] = parts


def unpack(core_ref, packed, field_out, even_out, diag_out, send):
    core = core_ref[0]

    def wide(which, columns):
        return jnp.concatenate([packed[which * NY + y][:, columns] for y in range(NY)], axis=1)

    field = wide(core, slice(0, H))
    field_out[...] = field
    even_out[...] = wide(1 - core, slice(0, H))
    diag_out[...] = wide(core, slice(H, 2 * H))
    store_parts(send, field)


def next_field(parts, rows, field, diag, up, down):
    total = None
    for z in range(NZ):
        term = lax.dot_general(
            parts[z],
            rows[:, z * W : (z + 1) * W],
            (((1,), (1,)), ((), ())),
            preferred_element_type=F32,
        )
        total = term if total is None else total + term
    blended = total if total.shape[0] == B else total[:B] + total[B:]
    own = (diag[0:1] + (2.0 - CENTRE)) * field[...]
    return (own + blended - (up[...] + down[...])) * (1.0 / SCALE)


def step(parts, rows, field, diag, up, down, field_out, send):
    out = next_field(parts, rows, field, diag, up, down)
    field_out[...] = out
    store_parts(send, out)


def last_step(parts, rows, field, diag, up, down, f0, f1, f2, field_out, send):
    out = next_field(parts, rows, field, diag, up, down)
    field_out[...] = out
    fields = [f0[...], f1[...], f2[...], field[...], out]
    lane = lax.broadcasted_iota(jnp.int32, (B, 128), 1)
    table = jnp.zeros((B, 128), F32)
    for p, (i, j) in enumerate(PAIRS):
        table = jnp.where(lane == p, jnp.sum(fields[i] * fields[j], axis=1, keepdims=True), table)
    for k in range(NX * NC):
        send[k] = table


def add_up(tables, send):
    total = tables[0]
    for k in range(1, NX * NC):
        total = total + tables[k]
    for z in range(NZ):
        send[z] = total


def finish(row_ref, tables, f0, f1, f2, f3, f4, solution_out, residual_out):
    total = tables[0]
    for z in range(1, NZ):
        total = total + tables[z]
    gram = {}
    for p, (i, j) in enumerate(PAIRS):
        gram[i, j] = gram[j, i] = total[:, p : p + 1]

    def inner(a, c):
        total = None
        for j, cj in enumerate(c):
            part = None
            for i, ai in enumerate(a):
                term = gram[i, j] if ai is None else ai * gram[i, j]
                part = term if part is None else part + term
            part = part if cj is None else part * cj
            total = part if total is None else total + part
        return total

    def plus(a, c, scale):
        out = []
        for k in range(max(len(a), len(c))):
            if k >= len(c):
                out.append(a[k])
            elif k >= len(a):
                out.append(scale * c[k])
            else:
                out.append(a[k] + scale * c[k])
        return out

    def image(a):
        out = [CENTRE * x for x in a] + [jnp.zeros_like(a[0])]
        for k, x in enumerate(a):
            out[k + 1] = out[k + 1] + SCALE * x
        return out

    one = jnp.ones((B, 1), F32)
    source = [None]
    found = None
    residual = search = [one]
    rho = gram[0, 0]
    for iteration in range(2):
        image_one = image(search)
        alpha = rho / inner(source, image_one)
        interim = plus(residual, image_one, -alpha)
        image_two = image(interim)
        omega = inner(image_two, interim) / inner(image_two, image_two)
        if found is None:
            found = [alpha * x for x in search]
        else:
            found = plus(found, search, alpha)
        found = plus(found, interim, omega)
        residual = plus(interim, image_two, -omega)
        if iteration == 0:
            rho_next = inner(source, residual)
            beta = (rho_next / rho) * (alpha / omega)
            search = plus(residual, plus(search, image_one, -omega), beta)
            rho = rho_next
    fields = [f0, f1, f2, f3, f4]
    row = row_ref[0]

    def combine(a):
        wide = a[0] * fields[0][...]
        for k in range(1, len(a)):
            wide = wide + a[k] * fields[k][...]
        own = wide[:, :H]
        for y in range(1, NY):
            own = jnp.where(row == y, wide[:, y * H : (y + 1) * H], own)
        return own

    solution_out[...] = combine(found)
    residual_out[...] = combine(residual)


def even(field):
    return lax.ppermute(field, ("x", "c"), [(i, i ^ 1) for i in range(NX * NC)])


def odd(field):
    pairs = [(i, i + 1) for i in range(1, NX * NC - 1, 2)]
    return lax.ppermute(field, ("x", "c"), pairs + [(j, i) for i, j in pairs])


def on_device(source, coupling, diagonal):
    own = coupling[0]
    row, core = (lax.axis_index(axis).astype(jnp.int32).reshape(1) for axis in ("y", "c"))
    packed = jnp.concatenate([source[0], jnp.broadcast_to(diagonal, (B, H))], axis=1)
    packed = jnp.broadcast_to(packed[None], (NC * NY, B, 128))
    packed = lax.all_to_all(packed, ("c", "y"), 0, 0, tiled=True)
    own, packed = lax.optimization_barrier((own, packed))
    rows = lax.all_gather(own, "y", axis=0, tiled=True)
    shape = jax.ShapeDtypeStruct
    wide = shape((B, W), F32)
    sends = [shape((NZ, B if k < LOW_FROM else 2 * B, W), BF16) for k in range(STEPS)]
    field, up, diag, send = call(unpack, (wide, wide, wide, sends[0]), core, packed, smem=1)
    fields = [field]
    for k in range(STEPS):
        down = odd(field)
        if k > 0:
            up = even(field)
        parts = lax.all_to_all(send, "z", 0, 0, tiled=True)
        if k + 1 < STEPS:
            field, send = call(
                step, (wide, sends[k + 1]), parts, rows, field, diag, up, down,
                loose=(1,) if k == 0 else (),
            )
            fields.append(field)
        else:
            last, table = call(
                last_step,
                (wide, shape((NX * NC, B, 128), F32)),
                parts, rows, field, diag, up, down, *fields[:3],
            )
    table = lax.all_to_all(table, ("x", "c"), 0, 0, tiled=True)
    table = call(add_up, shape((NZ, B, 128), F32), table)
    table = lax.all_to_all(table, "z", 0, 0, tiled=True)
    own_shape = shape((B, H), F32)
    found, residual = call(
        finish, (own_shape, own_shape), row, table, *fields, last, smem=1, keep=False
    )
    return found[None], residual[None]


def solution(mesh):
    fine = Mesh(mesh.devices.reshape(NX, NC, NZ, NY), ("x", "c", "z", "y"))
    depth, harm = ("x", "c"), ("z", "y")
    return jax.shard_map(
        on_device,
        mesh=fine,
        in_specs=(P(depth, None, harm), P(depth, harm, None), P(depth, harm)),
        out_specs=(P(depth, None, harm), P(depth, None, harm)),
        check_vma=False,
    )
```

```python
import jax
import jax.numpy as jnp
from jax import lax
from jax.experimental import pallas as pl
from jax.experimental.pallas import tpu as pltpu
from jax.sharding import Mesh, PartitionSpec as P

STEPS = 4
LOW_FROM = 0
CENTRE = 6.75
SCALE = 32.0
PAIRS = [(i, j) for j in range(STEPS + 1) for i in range(j + 1)]
NZ, NY, NX, NC = 16, 4, 4, 2
B = 8
H = 64
W = NY * H
F32 = jnp.float32
BF16 = jnp.bfloat16


def call(body, outs, *args, smem=0, keep=True):
    args = args[:smem] + tuple(
        pltpu.with_memory_space_constraint(x, pltpu.VMEM) for x in args[smem:]
    )
    if keep:
        outs = jax.tree.map(lambda o: pltpu.VMEM(o.shape, o.dtype), outs)
    specs = [pl.BlockSpec(memory_space=pltpu.SMEM)] * smem
    specs += [pl.BlockSpec(memory_space=pltpu.VMEM)] * (len(args) - smem)
    return pl.pallas_call(
        body,
        out_shape=outs,
        in_specs=specs,
        compiler_params=pltpu.CompilerParams(vmem_limit_bytes=8 << 20),
        out_specs=jax.tree.map(lambda _: pl.BlockSpec(memory_space=pltpu.VMEM), outs),
    )(*args)


def store_parts(send, field, row):
    turned = pltpu.roll(field, row * H, 1)
    parts = turned.astype(BF16)
    if send.shape[1] > B:
        low = (turned - parts.astype(F32)).astype(BF16)
        parts = jnp.concatenate([parts, low], axis=0)
    for z in range(NZ):
        send[z] = parts


def unpack(row_ref, packed, field_out, even_out, diag_out, send):
    row = row_ref[0] % NY
    core = row_ref[0] // NY

    def wide(which, columns):
        joined = jnp.concatenate([packed[which * NY + y][:, columns] for y in range(NY)], axis=1)
        return pltpu.roll(joined, (NY - row) % NY * H, 1)

    field = wide(core, slice(0, H))
    field_out[...] = field
    even_out[...] = wide(1 - core, slice(0, H))
    diag_out[...] = wide(core, slice(H, 2 * H))
    store_parts(send, field, row)


def next_field(parts, blocks, field, diag, up, down):
    sums = []
    for block in blocks:
        total = None
        for z in range(NZ):
            term = lax.dot_general(
                parts[z],
                block[:, z * W : (z + 1) * W],
                (((1,), (1,)), ((), ())),
                preferred_element_type=F32,
            )
            total = term if total is None else total + term
        sums.append(total if total.shape[0] == B else total[:B] + total[B:])
    blended = jnp.concatenate(sums, axis=1)
    own = (diag[0:1] + (2.0 - CENTRE)) * field[...]
    return (own + blended - (up[...] + down[...])) * (1.0 / SCALE)


def step(row_ref, parts, c0, c1, c2, c3, c4, field, diag, up, down, field_out, send):
    out = next_field(parts, (c0, c1, c2, c3, c4), field, diag, up, down)
    field_out[...] = out
    store_parts(send, out, row_ref[0] % NY)


def last_step(parts, c0, c1, c2, c3, c4, field, diag, up, down, f0, f1, f2, field_out, send):
    out = next_field(parts, (c0, c1, c2, c3, c4), field, diag, up, down)
    field_out[...] = out[:, :H]
    fields = [f0[...], f1[...], f2[...], field[...], out]
    lane = lax.broadcasted_iota(jnp.int32, (B, 128), 1)
    table = jnp.zeros((B, 128), F32)
    for p, (i, j) in enumerate(PAIRS):
        table = jnp.where(lane == p, jnp.sum(fields[i] * fields[j], axis=1, keepdims=True), table)
    for k in range(NX * NC):
        send[k] = table


def add_up(tables, send):
    total = tables[0]
    for k in range(1, NX * NC):
        total = total + tables[k]
    for z in range(NZ):
        send[z] = total


def finish(tables, f0, f1, f2, f3, f4, solution_out, residual_out):
    total = tables[0]
    for z in range(1, NZ):
        total = total + tables[z]
    gram = {}
    for p, (i, j) in enumerate(PAIRS):
        gram[i, j] = gram[j, i] = total[:, p : p + 1]

    def inner(a, c):
        total = None
        for j, cj in enumerate(c):
            part = None
            for i, ai in enumerate(a):
                term = gram[i, j] if ai is None else ai * gram[i, j]
                part = term if part is None else part + term
            part = part if cj is None else part * cj
            total = part if total is None else total + part
        return total

    def plus(a, c, scale):
        out = []
        for k in range(max(len(a), len(c))):
            if k >= len(c):
                out.append(a[k])
            elif k >= len(a):
                out.append(scale * c[k])
            else:
                out.append(a[k] + scale * c[k])
        return out

    def image(a):
        out = [CENTRE * x for x in a] + [jnp.zeros_like(a[0])]
        for k, x in enumerate(a):
            out[k + 1] = out[k + 1] + SCALE * x
        return out

    one = jnp.ones((B, 1), F32)
    source = [None]
    found = None
    residual = search = [one]
    rho = gram[0, 0]
    for iteration in range(2):
        image_one = image(search)
        alpha = rho / inner(source, image_one)
        interim = plus(residual, image_one, -alpha)
        image_two = image(interim)
        omega = inner(image_two, interim) / inner(image_two, image_two)
        if found is None:
            found = [alpha * x for x in search]
        else:
            found = plus(found, search, alpha)
        found = plus(found, interim, omega)
        residual = plus(interim, image_two, -omega)
        if iteration == 0:
            rho_next = inner(source, residual)
            beta = (rho_next / rho) * (alpha / omega)
            search = plus(residual, plus(search, image_one, -omega), beta)
            rho = rho_next
    fields = [f0[:, :H], f1[:, :H], f2[:, :H], f3[:, :H], f4[...]]

    def combine(a):
        out = a[0] * fields[0]
        for k in range(1, len(a)):
            out = out + a[k] * fields[k]
        return out

    solution_out[...] = combine(found)
    residual_out[...] = combine(residual)


def shifted(array, shift):
    return lax.ppermute(array, "y", [((y + shift) % NY, y) for y in range(NY)])


def even(field):
    return lax.ppermute(field, ("x", "c"), [(i, i ^ 1) for i in range(NX * NC)])


def odd(field):
    pairs = [(i, i + 1) for i in range(1, NX * NC - 1, 2)]
    return lax.ppermute(field, ("x", "c"), pairs + [(j, i) for i, j in pairs])


def on_device(source, coupling, diagonal):
    own = coupling[0]
    row = lax.axis_index(("c", "y")).astype(jnp.int32).reshape(1)
    packed = jnp.concatenate([source[0], jnp.broadcast_to(diagonal, (B, H))], axis=1)
    packed = jnp.broadcast_to(packed[None], (NC * NY, B, 128))
    packed = lax.all_to_all(packed, ("c", "y"), 0, 0, tiled=True)
    own, packed = lax.optimization_barrier((own, packed))
    after, before = shifted(own, 1), shifted(own, -1)
    blocks = [own, after, shifted(after[: H // 2], 1), shifted(before[H // 2 :], -1), before]
    shape = jax.ShapeDtypeStruct
    wide = shape((B, W), F32)
    sends = [shape((NZ, B if k < LOW_FROM else 2 * B, W), BF16) for k in range(STEPS)]
    field, up, diag, send = call(unpack, (wide, wide, wide, sends[0]), row, packed, smem=1)
    fields = [field]
    for k in range(STEPS):
        down = odd(field)
        if k > 0:
            up = even(field)
        parts = lax.all_to_all(send, "z", 0, 0, tiled=True)
        if k + 1 < STEPS:
            field, send = call(
                step,
                (wide, sends[k + 1]),
                row, parts, *blocks, field, diag, up, down,
                smem=1,

            )
            fields.append(field)
        else:
            last, table = call(
                last_step,
                (shape((B, H), F32), shape((NX * NC, B, 128), F32)),
                parts, *blocks, field, diag, up, down, *fields[:3],
            )
    table = lax.all_to_all(table, ("x", "c"), 0, 0, tiled=True)
    table = call(add_up, shape((NZ, B, 128), F32), table)
    table = lax.all_to_all(table, "z", 0, 0, tiled=True)
    own_shape = shape((B, H), F32)
    found, residual = call(finish, (own_shape, own_shape), table, *fields, last, keep=False)
    return found[None], residual[None]


def solution(mesh):
    fine = Mesh(mesh.devices.reshape(NX, NC, NZ, NY), ("x", "c", "z", "y"))
    depth, harm = ("x", "c"), ("z", "y")
    return jax.shard_map(
        on_device,
        mesh=fine,
        in_specs=(P(depth, None, harm), P(depth, harm, None), P(depth, harm)),
        out_specs=(P(depth, None, harm), P(depth, None, harm)),
        check_vma=False,
    )
```

```python
import jax
import jax.numpy as jnp
from jax import lax
from jax.experimental import pallas as pl
from jax.experimental.pallas import tpu as pltpu
from jax.sharding import Mesh, PartitionSpec as P

STEPS = 4
CENTRE = 6.75
SCALE = 32.0
PAIRS = [(i, j) for j in range(STEPS + 1) for i in range(j + 1)]
NZ, NY, NX, NC = 16, 4, 4, 2
B = 8
H = 64
W = NY * H
F32 = jnp.float32
BF16 = jnp.bfloat16


def call(body, outs, *args, smem=0, keep=True):
    args = args[:smem] + tuple(
        pltpu.with_memory_space_constraint(x, pltpu.VMEM) for x in args[smem:]
    )
    if keep:
        outs = jax.tree.map(lambda o: pltpu.VMEM(o.shape, o.dtype), outs)
    specs = [pl.BlockSpec(memory_space=pltpu.SMEM)] * smem
    specs += [pl.BlockSpec(memory_space=pltpu.VMEM)] * (len(args) - smem)
    return pl.pallas_call(
        body,
        out_shape=outs,
        in_specs=specs,
        compiler_params=pltpu.CompilerParams(vmem_limit_bytes=8 << 20),
        out_specs=jax.tree.map(lambda _: pl.BlockSpec(memory_space=pltpu.VMEM), outs),
    )(*args)


def store_parts(send, field, row):
    turned = pltpu.roll(field, row * H, 1)
    high = turned.astype(BF16)
    low = (turned - high.astype(F32)).astype(BF16)
    both = jnp.concatenate([high, low], axis=0)
    for z in range(NZ):
        send[z] = both


def unpack(row_ref, packed, field_out, even_out, diag_out, send):
    row = row_ref[0] % NY
    core = row_ref[0] // NY % NC

    def wide(which, columns):
        joined = jnp.concatenate([packed[which * NY + y][:, columns] for y in range(NY)], axis=1)
        return pltpu.roll(joined, (NY - row) % NY * H, 1)

    field = wide(core, slice(0, H))
    field_out[...] = field
    even_out[...] = wide(1 - core, slice(0, H))
    diag_out[...] = wide(core, slice(H, 2 * H))
    store_parts(send, field, row)


def next_field(parts, blocks, field, diag, beside):
    sums = []
    for block in blocks:
        total = None
        for z in range(NZ):
            term = lax.dot_general(
                parts[z],
                block[:, z * W : (z + 1) * W],
                (((1,), (1,)), ((), ())),
                preferred_element_type=F32,
            )
            total = term if total is None else total + term
        sums.append(total[:B] + total[B:])
    blended = jnp.concatenate(sums, axis=1)
    own = (diag[0:1] + (2.0 - CENTRE)) * field[...]
    total = own + blended
    if beside is not None:
        total = total - beside
    return total * (1.0 / SCALE)


def step(row_ref, parts, c0, c1, c2, c3, c4, field, diag, up, down, field_out, send):
    out = next_field(parts, (c0, c1, c2, c3, c4), field, diag, up[...] + down[...])
    field_out[...] = out
    store_parts(send, out, row_ref[0] % NY)


def last_step(parts, c0, c1, c2, c3, c4, field, diag, f0, f1, f2, u0, d0, u1, d1, u2, d2, send):
    partial = next_field(parts, (c0, c1, c2, c3, c4), field, diag, None)
    f3 = field[...]
    fields = [f0[...], f1[...], f2[...], f3]
    beside = [u0[...] + d0[...], u1[...] + d1[...], u2[...] + d2[...]]
    lane = lax.broadcasted_iota(jnp.int32, (B, 128), 1)
    table = jnp.zeros((B, 128), F32)
    for p, (i, j) in enumerate(PAIRS):
        if j < STEPS:
            terms = fields[i] * fields[j]
        elif i < STEPS - 1:
            terms = partial * fields[i] - f3 * beside[i] * (1.0 / SCALE)
        else:
            continue
        table = jnp.where(lane == p, jnp.sum(terms, axis=1, keepdims=True), table)
    packed = jnp.concatenate([table, partial, f3], axis=1)
    for k in range(NX * NC):
        send[k] = packed


def add_up(plane_ref, packed, last_out, send):
    count = NX * NC
    inv = 1.0 / SCALE

    def partial(p):
        return packed[p][:, 128 : 128 + W]

    def before(p):
        return packed[p][:, 128 + W :]

    table = packed[0][:, :128]
    for p in range(1, count):
        table = table + packed[p][:, :128]
    square = cross = jnp.zeros((B, W), F32)
    for p in range(count):
        beside = before(p - 1) if p > 0 else 0.0
        if p + 1 < count:
            beside = beside + before(p + 1)
        last = partial(p) - beside * inv
        square = square + last * last
        cross = cross + last * before(p)
    lane = lax.broadcasted_iota(jnp.int32, (B, 128), 1)
    for pair, terms in (((STEPS - 1, STEPS), cross), ((STEPS, STEPS), square)):
        value = jnp.sum(terms, axis=1, keepdims=True)
        table = jnp.where(lane == PAIRS.index(pair), value, table)
    for z in range(NZ):
        send[z] = table
    plane = plane_ref[0] // NY
    above = jnp.where(plane > 0, before(jnp.maximum(plane - 1, 0)), 0.0)
    below = jnp.where(plane + 1 < count, before(jnp.minimum(plane + 1, count - 1)), 0.0)
    last_out[...] = partial(plane) - (above + below) * inv


def finish(tables, f0, f1, f2, f3, f4, solution_out, residual_out):
    total = tables[0]
    for z in range(1, NZ):
        total = total + tables[z]
    gram = {}
    for p, (i, j) in enumerate(PAIRS):
        gram[i, j] = gram[j, i] = total[:, p : p + 1]

    def inner(a, c):
        total = None
        for j, cj in enumerate(c):
            part = None
            for i, ai in enumerate(a):
                term = gram[i, j] if ai is None else ai * gram[i, j]
                part = term if part is None else part + term
            part = part if cj is None else part * cj
            total = part if total is None else total + part
        return total

    def plus(a, c, scale):
        out = []
        for k in range(max(len(a), len(c))):
            if k >= len(c):
                out.append(a[k])
            elif k >= len(a):
                out.append(scale * c[k])
            else:
                out.append(a[k] + scale * c[k])
        return out

    def image(a):
        out = [CENTRE * x for x in a] + [jnp.zeros_like(a[0])]
        for k, x in enumerate(a):
            out[k + 1] = out[k + 1] + SCALE * x
        return out

    one = jnp.ones((B, 1), F32)
    source = [None]
    found = None
    residual = search = [one]
    rho = gram[0, 0]
    for iteration in range(2):
        image_one = image(search)
        alpha = rho / inner(source, image_one)
        interim = plus(residual, image_one, -alpha)
        image_two = image(interim)
        omega = inner(image_two, interim) / inner(image_two, image_two)
        if found is None:
            found = [alpha * x for x in search]
        else:
            found = plus(found, search, alpha)
        found = plus(found, interim, omega)
        residual = plus(interim, image_two, -omega)
        if iteration == 0:
            rho_next = inner(source, residual)
            beta = (rho_next / rho) * (alpha / omega)
            search = plus(residual, plus(search, image_one, -omega), beta)
            rho = rho_next
    fields = [f[:, :H] for f in (f0, f1, f2, f3, f4)]

    def combine(a):
        out = a[0] * fields[0]
        for k in range(1, len(a)):
            out = out + a[k] * fields[k]
        return out

    solution_out[...] = combine(found)
    residual_out[...] = combine(residual)


def shifted(array, shift):
    return lax.ppermute(array, "y", [((y + shift) % NY, y) for y in range(NY)])


def even(field):
    return lax.ppermute(field, ("x", "c"), [(i, i ^ 1) for i in range(NX * NC)])


def odd(field):
    pairs = [(i, i + 1) for i in range(1, NX * NC - 1, 2)]
    return lax.ppermute(field, ("x", "c"), pairs + [(j, i) for i, j in pairs])


def on_device(source, coupling, diagonal):
    own = coupling[0]
    row = lax.axis_index(("x", "c", "y")).astype(jnp.int32).reshape(1)
    packed = jnp.concatenate([source[0], jnp.broadcast_to(diagonal, (B, H))], axis=1)
    packed = jnp.broadcast_to(packed[None], (NC * NY, B, 128))
    packed = lax.all_to_all(packed, ("c", "y"), 0, 0, tiled=True)
    own, packed = lax.optimization_barrier((own, packed))
    after, before = shifted(own, 1), shifted(own, -1)
    blocks = [own, after, shifted(after[: H // 2], 1), shifted(before[H // 2 :], -1), before]
    shape = jax.ShapeDtypeStruct
    wide = shape((B, W), F32)
    send_shape = shape((NZ, 2 * B, W), BF16)
    field, up, diag, send = call(unpack, (wide, wide, wide, send_shape), row, packed, smem=1)
    fields, beside = [field], []
    for k in range(STEPS - 1):
        down = odd(field)
        if k > 0:
            up = even(field)
        beside += [up, down]
        parts = lax.all_to_all(send, "z", 0, 0, tiled=True)
        field, send = call(
            step, (wide, send_shape), row, parts, *blocks, field, diag, up, down, smem=1
        )
        fields.append(field)
    parts = lax.all_to_all(send, "z", 0, 0, tiled=True)
    packed = call(
        last_step,
        shape((NX * NC, B, 128 + 2 * W), F32),
        parts, *blocks, field, diag, *fields[:3], *beside,
    )
    packed = lax.all_to_all(packed, ("x", "c"), 0, 0, tiled=True)
    last, table = call(add_up, (wide, shape((NZ, B, 128), F32)), row, packed, smem=1)
    table = lax.all_to_all(table, "z", 0, 0, tiled=True)
    own_shape = shape((B, H), F32)
    found, residual = call(finish, (own_shape, own_shape), table, *fields, last, keep=False)
    return found[None], residual[None]


def solution(mesh):
    fine = Mesh(mesh.devices.reshape(NX, NC, NZ, NY), ("x", "c", "z", "y"))
    depth, harm = ("x", "c"), ("z", "y")
    return jax.shard_map(
        on_device,
        mesh=fine,
        in_specs=(P(depth, None, harm), P(depth, harm, None), P(depth, harm)),
        out_specs=(P(depth, None, harm), P(depth, None, harm)),
        check_vma=False,
    )
```

```python
import jax
import jax.numpy as jnp
from jax import lax
from jax.experimental import pallas as pl
from jax.experimental.pallas import tpu as pltpu
from jax.sharding import Mesh, PartitionSpec as P

STEPS = 4
CENTRE = 6.75
SCALE = 32.0
LINK = (6.5**2 / 12 + 2.0) / SCALE
WITH_LOW = (True, True, True, False)
PAIRS = [(i, j) for j in range(STEPS + 1) for i in range(j + 1)]
NZ, NY, NX, NC = 16, 4, 4, 2
B = 8
H = 64
W = NY * H
F32 = jnp.float32
BF16 = jnp.bfloat16


def call(body, outs, *args, smem=0, keep=True):
    args = args[:smem] + tuple(
        pltpu.with_memory_space_constraint(x, pltpu.VMEM) for x in args[smem:]
    )
    if keep:
        outs = jax.tree.map(lambda o: pltpu.VMEM(o.shape, o.dtype), outs)
    specs = [pl.BlockSpec(memory_space=pltpu.SMEM)] * smem
    specs += [pl.BlockSpec(memory_space=pltpu.VMEM)] * (len(args) - smem)
    return pl.pallas_call(
        body,
        out_shape=outs,
        in_specs=specs,
        compiler_params=pltpu.CompilerParams(vmem_limit_bytes=8 << 20),
        out_specs=jax.tree.map(lambda _: pl.BlockSpec(memory_space=pltpu.VMEM), outs),
    )(*args)


def store_parts(send, field, row):
    turned = pltpu.roll(field, row * H, 1)
    parts = turned.astype(BF16)
    if send.shape[1] > B:
        low = (turned - parts.astype(F32)).astype(BF16)
        parts = jnp.concatenate([parts, low], axis=0)
    for z in range(NZ):
        send[z] = parts


def unpack(row_ref, packed, field_out, even_out, diag_out, send):
    row = row_ref[0] % NY
    core = row_ref[0] // NY % NC

    def wide(which, columns):
        joined = jnp.concatenate([packed[which * NY + y][:, columns] for y in range(NY)], axis=1)
        return pltpu.roll(joined, (NY - row) % NY * H, 1)

    field = wide(core, slice(0, H))
    field_out[...] = field
    even_out[...] = wide(1 - core, slice(0, H))
    diag_out[...] = wide(core, slice(H, 2 * H))
    store_parts(send, field, row)


def next_field(parts, blocks, field, previous, diag, beside):
    sums = []
    for block in blocks:
        total = None
        for z in range(NZ):
            term = lax.dot_general(
                parts[z],
                block[:, z * W : (z + 1) * W],
                (((1,), (1,)), ((), ())),
                preferred_element_type=F32,
            )
            total = term if total is None else total + term
        sums.append(total if total.shape[0] == B else total[:B] + total[B:])
    blended = jnp.concatenate(sums, axis=1)
    own = (diag[0:1] + (2.0 - CENTRE)) * field[...]
    total = own + blended
    if previous is not None:
        total = total - LINK * previous[...]
    if beside is not None:
        total = total - beside
    return total * (1.0 / SCALE)


def step(row_ref, parts, c0, c1, c2, c3, c4, diag, up, down, field, *rest):
    *previous, field_out, send = rest
    previous = previous[0] if previous else None
    out = next_field(parts, (c0, c1, c2, c3, c4), field, previous, diag, up[...] + down[...])
    field_out[...] = out
    store_parts(send, out, row_ref[0] % NY)


def last_step(parts, c0, c1, c2, c3, c4, field, diag, f0, f1, f2, u0, d0, u1, d1, u2, d2, send):
    partial = next_field(parts, (c0, c1, c2, c3, c4), field, f2, diag, None)
    f3 = field[...]
    fields = [f0[...], f1[...], f2[...], f3]
    beside = [u0[...] + d0[...], u1[...] + d1[...], u2[...] + d2[...]]
    lane = lax.broadcasted_iota(jnp.int32, (B, 128), 1)
    table = jnp.zeros((B, 128), F32)
    for p, (i, j) in enumerate(PAIRS):
        if j < STEPS:
            terms = fields[i] * fields[j]
        elif i < STEPS - 1:
            terms = partial * fields[i] - f3 * beside[i] * (1.0 / SCALE)
        else:
            continue
        table = jnp.where(lane == p, jnp.sum(terms, axis=1, keepdims=True), table)
    packed = jnp.concatenate([table, partial, f3], axis=1)
    for k in range(NX * NC):
        send[k] = packed


def add_up(plane_ref, packed, last_out, send):
    count = NX * NC
    inv = 1.0 / SCALE

    def partial(p):
        return packed[p][:, 128 : 128 + W]

    def before(p):
        return packed[p][:, 128 + W :]

    table = packed[0][:, :128]
    for p in range(1, count):
        table = table + packed[p][:, :128]
    square = cross = jnp.zeros((B, W), F32)
    for p in range(count):
        beside = before(p - 1) if p > 0 else 0.0
        if p + 1 < count:
            beside = beside + before(p + 1)
        last = partial(p) - beside * inv
        square = square + last * last
        cross = cross + last * before(p)
    lane = lax.broadcasted_iota(jnp.int32, (B, 128), 1)
    for pair, terms in (((STEPS - 1, STEPS), cross), ((STEPS, STEPS), square)):
        value = jnp.sum(terms, axis=1, keepdims=True)
        table = jnp.where(lane == PAIRS.index(pair), value, table)
    for z in range(NZ):
        send[z] = table
    plane = plane_ref[0] // NY
    above = jnp.where(plane > 0, before(jnp.maximum(plane - 1, 0)), 0.0)
    below = jnp.where(plane + 1 < count, before(jnp.minimum(plane + 1, count - 1)), 0.0)
    last_out[...] = partial(plane) - (above + below) * inv


def finish(tables, f0, f1, f2, f3, f4, solution_out, residual_out):
    total = tables[0]
    for z in range(1, NZ):
        total = total + tables[z]
    gram = {}
    for p, (i, j) in enumerate(PAIRS):
        gram[i, j] = gram[j, i] = total[:, p : p + 1]

    def inner(a, c):
        total = None
        for j, cj in enumerate(c):
            part = None
            for i, ai in enumerate(a):
                term = gram[i, j] if ai is None else ai * gram[i, j]
                part = term if part is None else part + term
            part = part if cj is None else part * cj
            total = part if total is None else total + part
        return total

    def plus(a, c, scale):
        out = []
        for k in range(max(len(a), len(c))):
            if k >= len(c):
                out.append(a[k])
            elif k >= len(a):
                out.append(scale * c[k])
            else:
                out.append(a[k] + scale * c[k])
        return out

    def image(a):
        out = [CENTRE * x for x in a] + [jnp.zeros_like(a[0])]
        for k, x in enumerate(a):
            out[k + 1] = out[k + 1] + SCALE * x
            if k > 0:
                out[k - 1] = out[k - 1] + LINK * x
        return out

    one = jnp.ones((B, 1), F32)
    source = [None]
    found = None
    residual = search = [one]
    rho = gram[0, 0]
    for iteration in range(2):
        image_one = image(search)
        alpha = rho / inner(source, image_one)
        interim = plus(residual, image_one, -alpha)
        image_two = image(interim)
        omega = inner(image_two, interim) / inner(image_two, image_two)
        if found is None:
            found = [alpha * x for x in search]
        else:
            found = plus(found, search, alpha)
        found = plus(found, interim, omega)
        residual = plus(interim, image_two, -omega)
        if iteration == 0:
            rho_next = inner(source, residual)
            beta = (rho_next / rho) * (alpha / omega)
            search = plus(residual, plus(search, image_one, -omega), beta)
            rho = rho_next
    fields = [f[:, :H] for f in (f0, f1, f2, f3, f4)]

    def combine(a):
        out = a[0] * fields[0]
        for k in range(1, len(a)):
            out = out + a[k] * fields[k]
        return out

    solution_out[...] = combine(found)
    residual_out[...] = combine(residual)


def shifted(array, shift):
    return lax.ppermute(array, "y", [((y + shift) % NY, y) for y in range(NY)])


def even(field):
    return lax.ppermute(field, ("x", "c"), [(i, i ^ 1) for i in range(NX * NC)])


def odd(field):
    pairs = [(i, i + 1) for i in range(1, NX * NC - 1, 2)]
    return lax.ppermute(field, ("x", "c"), pairs + [(j, i) for i, j in pairs])


def on_device(source, coupling, diagonal):
    own = coupling[0]
    row = lax.axis_index(("x", "c", "y")).astype(jnp.int32).reshape(1)
    packed = jnp.concatenate([source[0], jnp.broadcast_to(diagonal, (B, H))], axis=1)
    packed = jnp.broadcast_to(packed[None], (NC * NY, B, 128))
    packed = lax.all_to_all(packed, ("c", "y"), 0, 0, tiled=True)
    own, packed = lax.optimization_barrier((own, packed))
    after, before = shifted(own, 1), shifted(own, -1)
    blocks = [own, after, shifted(after[: H // 2], 1), shifted(before[H // 2 :], -1), before]
    shape = jax.ShapeDtypeStruct
    wide = shape((B, W), F32)
    sends = [shape((NZ, 2 * B if low else B, W), BF16) for low in WITH_LOW]
    field, up, diag, send = call(unpack, (wide, wide, wide, sends[0]), row, packed, smem=1)
    fields, beside = [field], []
    for k in range(STEPS - 1):
        down = odd(field)
        if k > 0:
            up = even(field)
        beside += [up, down]
        parts = lax.all_to_all(send, "z", 0, 0, tiled=True)
        field, send = call(
            step,
            (wide, sends[k + 1]),
            row, parts, *blocks, diag, up, down, *fields[::-1][:2],
            smem=1,
        )
        fields.append(field)
    parts = lax.all_to_all(send, "z", 0, 0, tiled=True)
    packed = call(
        last_step,
        shape((NX * NC, B, 128 + 2 * W), F32),
        parts, *blocks, field, diag, *fields[:3], *beside,
    )
    packed = lax.all_to_all(packed, ("x", "c"), 0, 0, tiled=True)
    last, table = call(add_up, (wide, shape((NZ, B, 128), F32)), row, packed, smem=1)
    table = lax.all_to_all(table, "z", 0, 0, tiled=True)
    own_shape = shape((B, H), F32)
    found, residual = call(finish, (own_shape, own_shape), table, *fields, last, keep=False)
    return found[None], residual[None]


def solution(mesh):
    fine = Mesh(mesh.devices.reshape(NX, NC, NZ, NY), ("x", "c", "z", "y"))
    depth, harm = ("x", "c"), ("z", "y")
    return jax.shard_map(
        on_device,
        mesh=fine,
        in_specs=(P(depth, None, harm), P(depth, harm, None), P(depth, harm)),
        out_specs=(P(depth, None, harm), P(depth, None, harm)),
        check_vma=False,
    )
```

```python
import jax
import jax.numpy as jnp
from jax import lax
from jax.experimental import pallas as pl
from jax.experimental.pallas import tpu as pltpu
from jax.sharding import Mesh, PartitionSpec as P

STEPS = 4
CENTRE = 6.75
SCALE = 32.0
LINK = (6.5**2 / 12 + 2.0) / SCALE
WITH_LOW = (True, True, True, False)
PAIRS = [(i, j) for j in range(STEPS + 1) for i in range(j + 1)]
NZ, NY, NX, NC = 16, 4, 4, 2
B = 8
H = 64
W = NY * H
F32 = jnp.float32
BF16 = jnp.bfloat16


def call(body, outs, *args, smem=0, loose=(), keep=True):
    args = args[:smem] + tuple(
        x if i in loose else pltpu.with_memory_space_constraint(x, pltpu.VMEM)
        for i, x in enumerate(args[smem:])
    )
    if keep:
        outs = jax.tree.map(lambda o: pltpu.VMEM(o.shape, o.dtype), outs)
    specs = [pl.BlockSpec(memory_space=pltpu.SMEM)] * smem
    specs += [pl.BlockSpec(memory_space=pltpu.VMEM)] * (len(args) - smem)
    return pl.pallas_call(
        body,
        out_shape=outs,
        in_specs=specs,
        compiler_params=pltpu.CompilerParams(vmem_limit_bytes=8 << 20),
        out_specs=jax.tree.map(lambda _: pl.BlockSpec(memory_space=pltpu.VMEM), outs),
    )(*args)


def reorder(field, row):
    lane = lax.broadcasted_iota(jnp.int32, field.shape, 1)
    pairs = jnp.where(lane % (2 * H) < H, pltpu.roll(field, W - H, 1), pltpu.roll(field, H, 1))
    field = jnp.where(row % 2 == 1, pairs, field)
    return jnp.where(row >= 2, pltpu.roll(field, 2 * H, 1), field)


def store_parts(send, field, row):
    turned = reorder(field, row)
    parts = turned.astype(BF16)
    if send.shape[1] > B:
        low = (turned - parts.astype(F32)).astype(BF16)
        parts = jnp.concatenate([parts, low], axis=0)
    for z in range(NZ):
        send[z] = parts


def unpack(row_ref, packed, field_out, even_out, diag_out, send):
    row = row_ref[0] % NY
    core = row_ref[0] // NY % NC

    def wide(which, columns):
        return reorder(
            jnp.concatenate([packed[which * NY + y][:, columns] for y in range(NY)], axis=1), row
        )

    field = wide(core, slice(0, H))
    field_out[...] = field
    even_out[...] = wide(1 - core, slice(0, H))
    diag_out[...] = wide(core, slice(H, 2 * H))
    store_parts(send, field, row)


def next_field(parts, blocks, field, previous, diag, beside):
    sums = []
    for block in blocks:
        total = None
        for z in range(NZ):
            term = lax.dot_general(
                parts[z],
                block[:, z * W : (z + 1) * W],
                (((1,), (1,)), ((), ())),
                preferred_element_type=F32,
            )
            total = term if total is None else total + term
        sums.append(total if total.shape[0] == B else total[:B] + total[B:])
    blended = jnp.concatenate(sums, axis=1)
    own = (diag[0:1] + (2.0 - CENTRE)) * field[...]
    total = own + blended
    if previous is not None:
        total = total - LINK * previous[...]
    if beside is not None:
        total = total - beside
    return total * (1.0 / SCALE)


def step(row_ref, parts, c0, c1, c2, c3, diag, up, down, field, *rest):
    *previous, field_out, send = rest
    previous = previous[0] if previous else None
    out = next_field(parts, (c0, c1, c2, c3), field, previous, diag, up[...] + down[...])
    field_out[...] = out
    store_parts(send, out, row_ref[0] % NY)


def last_step(parts, c0, c1, c2, c3, field, diag, f0, f1, f2, u0, d0, u1, d1, u2, d2, send):
    partial = next_field(parts, (c0, c1, c2, c3), field, f2, diag, None)
    f3 = field[...]
    fields = [f0[...], f1[...], f2[...], f3]
    beside = [u0[...] + d0[...], u1[...] + d1[...], u2[...] + d2[...]]
    lane = lax.broadcasted_iota(jnp.int32, (B, 128), 1)
    table = jnp.zeros((B, 128), F32)
    for p, (i, j) in enumerate(PAIRS):
        if j < STEPS:
            terms = fields[i] * fields[j]
        elif i < STEPS - 1:
            terms = partial * fields[i] - f3 * beside[i] * (1.0 / SCALE)
        else:
            continue
        table = jnp.where(lane == p, jnp.sum(terms, axis=1, keepdims=True), table)
    packed = jnp.concatenate([table, partial, f3], axis=1)
    for k in range(NX * NC):
        send[k] = packed


def add_up(plane_ref, packed, last_out, send):
    count = NX * NC
    inv = 1.0 / SCALE

    def partial(p):
        return packed[p][:, 128 : 128 + W]

    def before(p):
        return packed[p][:, 128 + W :]

    table = packed[0][:, :128]
    for p in range(1, count):
        table = table + packed[p][:, :128]
    square = cross = jnp.zeros((B, W), F32)
    for p in range(count):
        beside = before(p - 1) if p > 0 else 0.0
        if p + 1 < count:
            beside = beside + before(p + 1)
        last = partial(p) - beside * inv
        square = square + last * last
        cross = cross + last * before(p)
    lane = lax.broadcasted_iota(jnp.int32, (B, 128), 1)
    for pair, terms in (((STEPS - 1, STEPS), cross), ((STEPS, STEPS), square)):
        value = jnp.sum(terms, axis=1, keepdims=True)
        table = jnp.where(lane == PAIRS.index(pair), value, table)
    for z in range(NZ):
        send[z] = table
    plane = plane_ref[0] // NY
    above = jnp.where(plane > 0, before(jnp.maximum(plane - 1, 0)), 0.0)
    below = jnp.where(plane + 1 < count, before(jnp.minimum(plane + 1, count - 1)), 0.0)
    last_out[...] = partial(plane) - (above + below) * inv


def finish(tables, f0, f1, f2, f3, f4, solution_out, residual_out):
    total = tables[0]
    for z in range(1, NZ):
        total = total + tables[z]
    gram = {}
    for p, (i, j) in enumerate(PAIRS):
        gram[i, j] = gram[j, i] = total[:, p : p + 1]

    def inner(a, c):
        total = None
        for j, cj in enumerate(c):
            part = None
            for i, ai in enumerate(a):
                term = gram[i, j] if ai is None else ai * gram[i, j]
                part = term if part is None else part + term
            part = part if cj is None else part * cj
            total = part if total is None else total + part
        return total

    def plus(a, c, scale):
        out = []
        for k in range(max(len(a), len(c))):
            if k >= len(c):
                out.append(a[k])
            elif k >= len(a):
                out.append(scale * c[k])
            else:
                out.append(a[k] + scale * c[k])
        return out

    def image(a):
        out = [CENTRE * x for x in a] + [jnp.zeros_like(a[0])]
        for k, x in enumerate(a):
            out[k + 1] = out[k + 1] + SCALE * x
            if k > 0:
                out[k - 1] = out[k - 1] + LINK * x
        return out

    one = jnp.ones((B, 1), F32)
    source = [None]
    found = None
    residual = search = [one]
    rho = gram[0, 0]
    for iteration in range(2):
        image_one = image(search)
        alpha = rho / inner(source, image_one)
        interim = plus(residual, image_one, -alpha)
        image_two = image(interim)
        omega = inner(image_two, interim) / inner(image_two, image_two)
        if found is None:
            found = [alpha * x for x in search]
        else:
            found = plus(found, search, alpha)
        found = plus(found, interim, omega)
        residual = plus(interim, image_two, -omega)
        if iteration == 0:
            rho_next = inner(source, residual)
            beta = (rho_next / rho) * (alpha / omega)
            search = plus(residual, plus(search, image_one, -omega), beta)
            rho = rho_next
    fields = [f[:, :H] for f in (f0, f1, f2, f3, f4)]

    def combine(a):
        out = a[0] * fields[0]
        for k in range(1, len(a)):
            out = out + a[k] * fields[k]
        return out

    solution_out[...] = combine(found)
    residual_out[...] = combine(residual)


def swapped(array, mask):
    return lax.ppermute(array, "y", [(y, y ^ mask) for y in range(NY)])


def even(field):
    return lax.ppermute(field, ("x", "c"), [(i, i ^ 1) for i in range(NX * NC)])


def odd(field):
    pairs = [(i, i + 1) for i in range(1, NX * NC - 1, 2)]
    return lax.ppermute(field, ("x", "c"), pairs + [(j, i) for i, j in pairs])


def on_device(source, coupling, diagonal):
    own = coupling[0]
    row = lax.axis_index(("x", "c", "y")).astype(jnp.int32).reshape(1)
    packed = jnp.concatenate([source[0], jnp.broadcast_to(diagonal, (B, H))], axis=1)
    packed = jnp.broadcast_to(packed[None], (NC * NY, B, 128))
    packed = lax.all_to_all(packed, ("c", "y"), 0, 0, tiled=True)
    by_1, by_3 = swapped(own, 1), swapped(own, 3)
    by_1, packed = lax.optimization_barrier((by_1, packed))
    blocks = [own, by_1, swapped(by_1, 3), by_3]
    shape = jax.ShapeDtypeStruct
    wide = shape((B, W), F32)
    sends = [shape((NZ, 2 * B if low else B, W), BF16) for low in WITH_LOW]
    field, up, diag, send = call(unpack, (wide, wide, wide, sends[0]), row, packed, smem=1)
    fields, beside = [field], []
    for k in range(STEPS - 1):
        down = odd(field)
        if k > 0:
            up = even(field)
        beside += [up, down]
        parts = lax.all_to_all(send, "z", 0, 0, tiled=True)
        field, send = call(
            step,
            (wide, sends[k + 1]),
            row, parts, *blocks, diag, up, down, *fields[::-1][:2],
            smem=1,
            loose=(1,) if k == 0 else (),
        )
        fields.append(field)
    parts = lax.all_to_all(send, "z", 0, 0, tiled=True)
    packed = call(
        last_step,
        shape((NX * NC, B, 128 + 2 * W), F32),
        parts, *blocks, field, diag, *fields[:3], *beside,
    )
    packed = lax.all_to_all(packed, ("x", "c"), 0, 0, tiled=True)
    last, table = call(add_up, (wide, shape((NZ, B, 128), F32)), row, packed, smem=1)
    table = lax.all_to_all(table, "z", 0, 0, tiled=True)
    own_shape = shape((B, H), F32)
    found, residual = call(finish, (own_shape, own_shape), table, *fields, last, keep=False)
    return found[None], residual[None]


def solution(mesh):
    fine = Mesh(mesh.devices.reshape(NX, NC, NZ, NY), ("x", "c", "z", "y"))
    depth, harm = ("x", "c"), ("z", "y")
    return jax.shard_map(
        on_device,
        mesh=fine,
        in_specs=(P(depth, None, harm), P(depth, harm, None), P(depth, harm)),
        out_specs=(P(depth, None, harm), P(depth, None, harm)),
        check_vma=False,
    )
```

```python
import jax
import jax.numpy as jnp
from jax import lax
from jax.experimental import pallas as pl
from jax.experimental.pallas import tpu as pltpu
from jax.sharding import Mesh, PartitionSpec as P

STEPS = 4
CENTRE = 6.75
SCALE = 32.0
LINK = (6.5**2 / 12 + 2.0) / SCALE
WITH_LOW = (True, True, True, False)
PAIRS = [(i, j) for j in range(STEPS + 1) for i in range(j + 1)]
NZ, NY, NX, NC = 16, 4, 4, 2
B = 8
H = 64
W = NY * H
F32 = jnp.float32
BF16 = jnp.bfloat16


def call(body, outs, *args, smem=0, keep=True, aliases={}):
    args = args[:smem] + tuple(
        pltpu.with_memory_space_constraint(x, pltpu.VMEM) for x in args[smem:]
    )
    if keep:
        outs = jax.tree.map(lambda o: pltpu.VMEM(o.shape, o.dtype), outs)
    specs = [pl.BlockSpec(memory_space=pltpu.SMEM)] * smem
    specs += [pl.BlockSpec(memory_space=pltpu.VMEM)] * (len(args) - smem)
    return pl.pallas_call(
        body,
        out_shape=outs,
        in_specs=specs,
        input_output_aliases=aliases,
        compiler_params=pltpu.CompilerParams(vmem_limit_bytes=8 << 20),
        out_specs=jax.tree.map(lambda _: pl.BlockSpec(memory_space=pltpu.VMEM), outs),
    )(*args)


def reorder(field, row):
    lane = lax.broadcasted_iota(jnp.int32, field.shape, 1)
    pairs = jnp.where(lane % (2 * H) < H, pltpu.roll(field, W - H, 1), pltpu.roll(field, H, 1))
    field = jnp.where(row % 2 == 1, pairs, field)
    return jnp.where(row >= 2, pltpu.roll(field, 2 * H, 1), field)


def store_parts(send, field, row):
    turned = reorder(field, row)
    parts = turned.astype(BF16)
    if send.shape[1] > B:
        low = (turned - parts.astype(F32)).astype(BF16)
        parts = jnp.concatenate([parts, low], axis=0)
    for z in range(NZ):
        send[z] = parts


def unpack(row_ref, packed, own, field_out, even_out, diag_out, send, own_out):
    row = row_ref[0] % NY
    core = row_ref[0] // NY % NC

    def wide(which, columns):
        return reorder(
            jnp.concatenate([packed[which * NY + y][:, columns] for y in range(NY)], axis=1), row
        )

    field = wide(core, slice(0, H))
    field_out[...] = field
    even_out[...] = wide(1 - core, slice(0, H))
    diag_out[...] = wide(core, slice(H, 2 * H))
    store_parts(send, field, row)


def next_field(parts, blocks, field, previous, diag, beside):
    sums = []
    for block in blocks:
        total = None
        for z in range(NZ):
            term = lax.dot_general(
                parts[z],
                block[:, z * W : (z + 1) * W],
                (((1,), (1,)), ((), ())),
                preferred_element_type=F32,
            )
            total = term if total is None else total + term
        sums.append(total if total.shape[0] == B else total[:B] + total[B:])
    blended = jnp.concatenate(sums, axis=1)
    own = (diag[0:1] + (2.0 - CENTRE)) * field[...]
    total = own + blended
    if previous is not None:
        total = total - LINK * previous[...]
    if beside is not None:
        total = total - beside
    return total * (1.0 / SCALE)


def step(row_ref, parts, c0, c1, c2, c3, diag, up, down, field, *rest):
    *previous, field_out, send = rest
    previous = previous[0] if previous else None
    out = next_field(parts, (c0, c1, c2, c3), field, previous, diag, up[...] + down[...])
    field_out[...] = out
    store_parts(send, out, row_ref[0] % NY)


def last_step(parts, c0, c1, c2, c3, field, diag, f0, f1, f2, u0, d0, u1, d1, u2, d2, send):
    partial = next_field(parts, (c0, c1, c2, c3), field, f2, diag, None)
    f3 = field[...]
    fields = [f0[...], f1[...], f2[...], f3]
    beside = [u0[...] + d0[...], u1[...] + d1[...], u2[...] + d2[...]]
    lane = lax.broadcasted_iota(jnp.int32, (B, 128), 1)
    table = jnp.zeros((B, 128), F32)
    for p, (i, j) in enumerate(PAIRS):
        if j < STEPS:
            terms = fields[i] * fields[j]
        elif i < STEPS - 1:
            terms = partial * fields[i] - f3 * beside[i] * (1.0 / SCALE)
        else:
            continue
        table = jnp.where(lane == p, jnp.sum(terms, axis=1, keepdims=True), table)
    packed = jnp.concatenate([table, partial, f3], axis=1)
    for k in range(NX * NC):
        send[k] = packed


def add_up(plane_ref, packed, last_out, send):
    count = NX * NC
    inv = 1.0 / SCALE

    def partial(p):
        return packed[p][:, 128 : 128 + W]

    def before(p):
        return packed[p][:, 128 + W :]

    table = packed[0][:, :128]
    for p in range(1, count):
        table = table + packed[p][:, :128]
    square = cross = jnp.zeros((B, W), F32)
    for p in range(count):
        beside = before(p - 1) if p > 0 else 0.0
        if p + 1 < count:
            beside = beside + before(p + 1)
        last = partial(p) - beside * inv
        square = square + last * last
        cross = cross + last * before(p)
    lane = lax.broadcasted_iota(jnp.int32, (B, 128), 1)
    for pair, terms in (((STEPS - 1, STEPS), cross), ((STEPS, STEPS), square)):
        value = jnp.sum(terms, axis=1, keepdims=True)
        table = jnp.where(lane == PAIRS.index(pair), value, table)
    for z in range(NZ):
        send[z] = table
    plane = plane_ref[0] // NY
    above = jnp.where(plane > 0, before(jnp.maximum(plane - 1, 0)), 0.0)
    below = jnp.where(plane + 1 < count, before(jnp.minimum(plane + 1, count - 1)), 0.0)
    last_out[...] = partial(plane) - (above + below) * inv


def finish(tables, f0, f1, f2, f3, f4, solution_out, residual_out):
    total = tables[0]
    for z in range(1, NZ):
        total = total + tables[z]
    gram = {}
    for p, (i, j) in enumerate(PAIRS):
        gram[i, j] = gram[j, i] = total[:, p : p + 1]

    def inner(a, c):
        total = None
        for j, cj in enumerate(c):
            part = None
            for i, ai in enumerate(a):
                term = gram[i, j] if ai is None else ai * gram[i, j]
                part = term if part is None else part + term
            part = part if cj is None else part * cj
            total = part if total is None else total + part
        return total

    def plus(a, c, scale):
        out = []
        for k in range(max(len(a), len(c))):
            if k >= len(c):
                out.append(a[k])
            elif k >= len(a):
                out.append(scale * c[k])
            else:
                out.append(a[k] + scale * c[k])
        return out

    def image(a):
        out = [CENTRE * x for x in a] + [jnp.zeros_like(a[0])]
        for k, x in enumerate(a):
            out[k + 1] = out[k + 1] + SCALE * x
            if k > 0:
                out[k - 1] = out[k - 1] + LINK * x
        return out

    one = jnp.ones((B, 1), F32)
    source = [None]
    found = None
    residual = search = [one]
    rho = gram[0, 0]
    for iteration in range(2):
        image_one = image(search)
        alpha = rho / inner(source, image_one)
        interim = plus(residual, image_one, -alpha)
        image_two = image(interim)
        omega = inner(image_two, interim) / inner(image_two, image_two)
        if found is None:
            found = [alpha * x for x in search]
        else:
            found = plus(found, search, alpha)
        found = plus(found, interim, omega)
        residual = plus(interim, image_two, -omega)
        if iteration == 0:
            rho_next = inner(source, residual)
            beta = (rho_next / rho) * (alpha / omega)
            search = plus(residual, plus(search, image_one, -omega), beta)
            rho = rho_next
    fields = [f[:, :H] for f in (f0, f1, f2, f3, f4)]

    def combine(a):
        out = a[0] * fields[0]
        for k in range(1, len(a)):
            out = out + a[k] * fields[k]
        return out

    solution_out[...] = combine(found)
    residual_out[...] = combine(residual)


def swapped(array, mask):
    return lax.ppermute(array, "y", [(y, y ^ mask) for y in range(NY)])


def even(field):
    return lax.ppermute(field, ("x", "c"), [(i, i ^ 1) for i in range(NX * NC)])


def odd(field):
    pairs = [(i, i + 1) for i in range(1, NX * NC - 1, 2)]
    return lax.ppermute(field, ("x", "c"), pairs + [(j, i) for i, j in pairs])


def on_device(source, coupling, diagonal):
    own = coupling[0]
    row = lax.axis_index(("x", "c", "y")).astype(jnp.int32).reshape(1)
    packed = jnp.concatenate([source[0], jnp.broadcast_to(diagonal, (B, H))], axis=1)
    packed = jnp.broadcast_to(packed[None], (NC * NY, B, 128))
    packed = lax.all_to_all(packed, ("c", "y"), 0, 0, tiled=True)
    by_1, by_3 = swapped(own, 1), swapped(own, 3)
    by_1, packed = lax.optimization_barrier((by_1, packed))
    by_2 = swapped(by_1, 3)
    shape = jax.ShapeDtypeStruct
    wide = shape((B, W), F32)
    sends = [shape((NZ, 2 * B if low else B, W), BF16) for low in WITH_LOW]
    field, up, diag, send, own = call(
        unpack,
        (wide, wide, wide, sends[0], shape((H, NZ * W), BF16)),
        row, packed, own,
        smem=1,
        aliases={2: 4},
    )
    blocks = [own, by_1, by_2, by_3]
    fields, beside = [field], []
    for k in range(STEPS - 1):
        down = odd(field)
        if k > 0:
            up = even(field)
        beside += [up, down]
        parts = lax.all_to_all(send, "z", 0, 0, tiled=True)
        field, send = call(
            step,
            (wide, sends[k + 1]),
            row, parts, *blocks, diag, up, down, *fields[::-1][:2],
            smem=1,
        )
        fields.append(field)
    parts = lax.all_to_all(send, "z", 0, 0, tiled=True)
    packed = call(
        last_step,
        shape((NX * NC, B, 128 + 2 * W), F32),
        parts, *blocks, field, diag, *fields[:3], *beside,
    )
    packed = lax.all_to_all(packed, ("x", "c"), 0, 0, tiled=True)
    last, table = call(add_up, (wide, shape((NZ, B, 128), F32)), row, packed, smem=1)
    table = lax.all_to_all(table, "z", 0, 0, tiled=True)
    own_shape = shape((B, H), F32)
    found, residual = call(finish, (own_shape, own_shape), table, *fields, last, keep=False)
    return found[None], residual[None]


def solution(mesh):
    fine = Mesh(mesh.devices.reshape(NX, NC, NZ, NY), ("x", "c", "z", "y"))
    depth, harm = ("x", "c"), ("z", "y")
    return jax.shard_map(
        on_device,
        mesh=fine,
        in_specs=(P(depth, None, harm), P(depth, harm, None), P(depth, harm)),
        out_specs=(P(depth, None, harm), P(depth, None, harm)),
        check_vma=False,
    )
```

```python
import jax
import jax.numpy as jnp
from jax import lax
from jax.experimental import pallas as pl
from jax.experimental.pallas import tpu as pltpu
from jax.sharding import Mesh, PartitionSpec as P

STEPS = 4
CENTRE = 6.75
SCALE = 32.0
LINK = (6.5**2 / 12 + 2.0) / SCALE
WITH_LOW = (False, True, True, False)
PAIRS = [(i, j) for j in range(STEPS + 1) for i in range(j + 1)]
NZ, NY, NX, NC = 16, 4, 4, 2
B = 8
H = 64
W = NY * H
F32 = jnp.float32
BF16 = jnp.bfloat16


def call(body, outs, *args, smem=0, hbm=0, scratch=(), keep=True):
    first = smem + hbm
    args = args[:smem] + tuple(
        pltpu.with_memory_space_constraint(x, pltpu.VMEM if i >= hbm else pltpu.HBM)
        for i, x in enumerate(args[smem:])
    )
    if keep:
        outs = jax.tree.map(lambda o: pltpu.VMEM(o.shape, o.dtype), outs)
    places = [pltpu.SMEM] * smem + [pltpu.HBM] * hbm + [pltpu.VMEM] * (len(args) - first)
    specs = [pl.BlockSpec(memory_space=place) for place in places]
    return pl.pallas_call(
        body,
        out_shape=outs,
        in_specs=specs,
        scratch_shapes=scratch,
        compiler_params=pltpu.CompilerParams(vmem_limit_bytes=8 << 20),
        out_specs=jax.tree.map(lambda _: pl.BlockSpec(memory_space=pltpu.VMEM), outs),
    )(*args)


def reorder(field, row):
    lane = lax.broadcasted_iota(jnp.int32, field.shape, 1)
    pairs = jnp.where(lane % (2 * H) < H, pltpu.roll(field, W - H, 1), pltpu.roll(field, H, 1))
    field = jnp.where(row % 2 == 1, pairs, field)
    return jnp.where(row >= 2, pltpu.roll(field, 2 * H, 1), field)


def store_parts(send, field, row):
    turned = reorder(field, row)
    parts = turned.astype(BF16)
    if send.shape[1] > B:
        low = (turned - parts.astype(F32)).astype(BF16)
        parts = jnp.concatenate([parts, low], axis=0)
    for z in range(NZ):
        send[z] = parts


def unpack(row_ref, packed, field_out, even_out, diag_out, send):
    row = row_ref[0] % NY
    core = row_ref[0] // NY % NC

    def wide(which, columns):
        return reorder(
            jnp.concatenate([packed[which * NY + y][:, columns] for y in range(NY)], axis=1), row
        )

    field = wide(core, slice(0, H))
    field_out[...] = field
    even_out[...] = wide(1 - core, slice(0, H))
    diag_out[...] = wide(core, slice(H, 2 * H))
    store_parts(send, field, row)


def next_field(parts, blocks, field, previous, diag, beside, wait=None):
    sums = []
    for block in blocks[::-1]:
        if wait is not None and block is blocks[0]:
            wait()
        total = None
        for z in range(NZ):
            term = lax.dot_general(
                parts[z],
                block[:, z * W : (z + 1) * W],
                (((1,), (1,)), ((), ())),
                preferred_element_type=F32,
            )
            total = term if total is None else total + term
        sums.append(total if total.shape[0] == B else total[:B] + total[B:])
    blended = jnp.concatenate(sums[::-1], axis=1)
    own = (diag[0:1] + (2.0 - CENTRE)) * field[...]
    total = own + blended
    if previous is not None:
        total = total - LINK * previous[...]
    if beside is not None:
        total = total - beside
    return total * (1.0 / SCALE)


def first_step(row_ref, own, parts, c1, c2, c3, diag, up, down, field, field_out, send, c0, arrived):
    fetch = pltpu.make_async_copy(own, c0, arrived)
    fetch.start()
    beside = up[...] + down[...]
    out = next_field(parts, (c0, c1, c2, c3), field, None, diag, beside, fetch.wait)
    field_out[...] = out
    store_parts(send, out, row_ref[0] % NY)


def step(row_ref, parts, c0, c1, c2, c3, diag, up, down, field, previous, field_out, send):
    out = next_field(parts, (c0, c1, c2, c3), field, previous, diag, up[...] + down[...])
    field_out[...] = out
    store_parts(send, out, row_ref[0] % NY)


def last_step(parts, c0, c1, c2, c3, field, diag, f0, f1, f2, u0, d0, u1, d1, u2, d2, send):
    partial = next_field(parts, (c0, c1, c2, c3), field, f2, diag, None)
    f3 = field[...]
    fields = [f0[...], f1[...], f2[...], f3]
    beside = [u0[...] + d0[...], u1[...] + d1[...], u2[...] + d2[...]]
    lane = lax.broadcasted_iota(jnp.int32, (B, 128), 1)
    table = jnp.zeros((B, 128), F32)
    for p, (i, j) in enumerate(PAIRS):
        if j < STEPS:
            terms = fields[i] * fields[j]
        elif i < STEPS - 1:
            terms = partial * fields[i] - f3 * beside[i] * (1.0 / SCALE)
        else:
            continue
        table = jnp.where(lane == p, jnp.sum(terms, axis=1, keepdims=True), table)
    packed = jnp.concatenate([table, partial, f3], axis=1)
    for k in range(NX * NC):
        send[k] = packed


def add_up(plane_ref, packed, last_out, send):
    count = NX * NC
    inv = 1.0 / SCALE

    def partial(p):
        return packed[p][:, 128 : 128 + W]

    def before(p):
        return packed[p][:, 128 + W :]

    table = packed[0][:, :128]
    for p in range(1, count):
        table = table + packed[p][:, :128]
    square = cross = jnp.zeros((B, W), F32)
    for p in range(count):
        beside = before(p - 1) if p > 0 else 0.0
        if p + 1 < count:
            beside = beside + before(p + 1)
        last = partial(p) - beside * inv
        square = square + last * last
        cross = cross + last * before(p)
    lane = lax.broadcasted_iota(jnp.int32, (B, 128), 1)
    for pair, terms in (((STEPS - 1, STEPS), cross), ((STEPS, STEPS), square)):
        value = jnp.sum(terms, axis=1, keepdims=True)
        table = jnp.where(lane == PAIRS.index(pair), value, table)
    for z in range(NZ):
        send[z] = table
    plane = plane_ref[0] // NY
    above = jnp.where(plane > 0, before(jnp.maximum(plane - 1, 0)), 0.0)
    below = jnp.where(plane + 1 < count, before(jnp.minimum(plane + 1, count - 1)), 0.0)
    last_out[...] = partial(plane) - (above + below) * inv


def finish(tables, f0, f1, f2, f3, f4, solution_out, residual_out):
    total = tables[0]
    for z in range(1, NZ):
        total = total + tables[z]
    gram = {}
    for p, (i, j) in enumerate(PAIRS):
        gram[i, j] = gram[j, i] = total[:, p : p + 1]

    def inner(a, c):
        total = None
        for j, cj in enumerate(c):
            part = None
            for i, ai in enumerate(a):
                term = gram[i, j] if ai is None else ai * gram[i, j]
                part = term if part is None else part + term
            part = part if cj is None else part * cj
            total = part if total is None else total + part
        return total

    def plus(a, c, scale):
        out = []
        for k in range(max(len(a), len(c))):
            if k >= len(c):
                out.append(a[k])
            elif k >= len(a):
                out.append(scale * c[k])
            else:
                out.append(a[k] + scale * c[k])
        return out

    def image(a):
        out = [CENTRE * x for x in a] + [jnp.zeros_like(a[0])]
        for k, x in enumerate(a):
            out[k + 1] = out[k + 1] + SCALE * x
            if k > 0:
                out[k - 1] = out[k - 1] + LINK * x
        return out

    one = jnp.ones((B, 1), F32)
    source = [None]
    found = None
    residual = search = [one]
    rho = gram[0, 0]
    for iteration in range(2):
        image_one = image(search)
        alpha = rho / inner(source, image_one)
        interim = plus(residual, image_one, -alpha)
        image_two = image(interim)
        omega = inner(image_two, interim) / inner(image_two, image_two)
        if found is None:
            found = [alpha * x for x in search]
        else:
            found = plus(found, search, alpha)
        found = plus(found, interim, omega)
        residual = plus(interim, image_two, -omega)
        if iteration == 0:
            rho_next = inner(source, residual)
            beta = (rho_next / rho) * (alpha / omega)
            search = plus(residual, plus(search, image_one, -omega), beta)
            rho = rho_next
    fields = [f[:, :H] for f in (f0, f1, f2, f3, f4)]

    def combine(a):
        out = a[0] * fields[0]
        for k in range(1, len(a)):
            out = out + a[k] * fields[k]
        return out

    solution_out[...] = combine(found)
    residual_out[...] = combine(residual)


def swapped(array, mask):
    return lax.ppermute(array, "y", [(y, y ^ mask) for y in range(NY)])


def even(field):
    return lax.ppermute(field, ("x", "c"), [(i, i ^ 1) for i in range(NX * NC)])


def odd(field):
    pairs = [(i, i + 1) for i in range(1, NX * NC - 1, 2)]
    return lax.ppermute(field, ("x", "c"), pairs + [(j, i) for i, j in pairs])


def on_device(source, coupling, diagonal):
    own = coupling[0]
    row = lax.axis_index(("x", "c", "y")).astype(jnp.int32).reshape(1)
    packed = jnp.concatenate([source[0], jnp.broadcast_to(diagonal, (B, H))], axis=1)
    packed = jnp.broadcast_to(packed[None], (NC * NY, B, 128))
    packed = lax.all_to_all(packed, ("c", "y"), 0, 0, tiled=True)
    by_1, by_3 = swapped(own, 1), swapped(own, 3)
    by_1, packed = lax.optimization_barrier((by_1, packed))
    blocks = [own, by_1, swapped(by_1, 3), by_3]
    shape = jax.ShapeDtypeStruct
    wide = shape((B, W), F32)
    sends = [shape((NZ, 2 * B if low else B, W), BF16) for low in WITH_LOW]
    field, up, diag, send = call(unpack, (wide, wide, wide, sends[0]), row, packed, smem=1)
    fields, beside = [field], []
    for k in range(STEPS - 1):
        down = odd(field)
        if k > 0:
            up = even(field)
        beside += [up, down]
        parts = lax.all_to_all(send, "z", 0, 0, tiled=True)
        outs = (wide, sends[k + 1])
        if k == 0:
            field, send = call(
                first_step, outs, row, own, parts, *blocks[1:], diag, up, down, field,
                smem=1,
                hbm=1,
                scratch=[pltpu.VMEM((H, NZ * W), BF16), pltpu.SemaphoreType.DMA],
            )
        else:
            field, send = call(
                step, outs, row, parts, *blocks, diag, up, down, *fields[::-1][:2], smem=1
            )
        fields.append(field)
    parts = lax.all_to_all(send, "z", 0, 0, tiled=True)
    packed = call(
        last_step,
        shape((NX * NC, B, 128 + 2 * W), F32),
        parts, *blocks, field, diag, *fields[:3], *beside,
    )
    packed = lax.all_to_all(packed, ("x", "c"), 0, 0, tiled=True)
    last, table = call(add_up, (wide, shape((NZ, B, 128), F32)), row, packed, smem=1)
    table = lax.all_to_all(table, "z", 0, 0, tiled=True)
    own_shape = shape((B, H), F32)
    found, residual = call(finish, (own_shape, own_shape), table, *fields, last, keep=False)
    return found[None], residual[None]


def solution(mesh):
    fine = Mesh(mesh.devices.reshape(NX, NC, NZ, NY), ("x", "c", "z", "y"))
    depth, harm = ("x", "c"), ("z", "y")
    return jax.shard_map(
        on_device,
        mesh=fine,
        in_specs=(P(depth, None, harm), P(depth, harm, None), P(depth, harm)),
        out_specs=(P(depth, None, harm), P(depth, None, harm)),
        check_vma=False,
    )
```

```python
import jax
import jax.numpy as jnp
from jax import lax
from jax.experimental import pallas as pl
from jax.experimental.pallas import tpu as pltpu
from jax.sharding import Mesh, PartitionSpec as P

STEPS = 4
CENTRE = 6.75
SCALE = 32.0
LINK = (6.5**2 / 12 + 2.0) / SCALE
WITH_LOW = (False, False, True, False)
PAIRS = [(i, j) for j in range(STEPS + 1) for i in range(j + 1)]
NZ, NY, NX, NC = 16, 4, 4, 2
B = 8
H = 64
W = NY * H
F32 = jnp.float32
BF16 = jnp.bfloat16


def call(body, outs, *args, smem=0, hbm=0, scratch=(), keep=True):
    first = smem + hbm
    args = args[:smem] + tuple(
        pltpu.with_memory_space_constraint(x, pltpu.VMEM if i >= hbm else pltpu.HBM)
        for i, x in enumerate(args[smem:])
    )
    if keep:
        outs = jax.tree.map(lambda o: pltpu.VMEM(o.shape, o.dtype), outs)
    places = [pltpu.SMEM] * smem + [pltpu.HBM] * hbm + [pltpu.VMEM] * (len(args) - first)
    specs = [pl.BlockSpec(memory_space=place) for place in places]
    return pl.pallas_call(
        body,
        out_shape=outs,
        in_specs=specs,
        scratch_shapes=scratch,
        compiler_params=pltpu.CompilerParams(vmem_limit_bytes=8 << 20),
        out_specs=jax.tree.map(lambda _: pl.BlockSpec(memory_space=pltpu.VMEM), outs),
    )(*args)


def reorder(field, row):
    lane = lax.broadcasted_iota(jnp.int32, field.shape, 1)
    pairs = jnp.where(lane % (2 * H) < H, pltpu.roll(field, W - H, 1), pltpu.roll(field, H, 1))
    field = jnp.where(row % 2 == 1, pairs, field)
    return jnp.where(row >= 2, pltpu.roll(field, 2 * H, 1), field)


def store_parts(send, field, row):
    turned = reorder(field, row)
    parts = turned.astype(BF16)
    if send.shape[1] > B:
        low = (turned - parts.astype(F32)).astype(BF16)
        parts = jnp.concatenate([parts, low], axis=0)
    for z in range(NZ):
        send[z] = parts


def unpack(row_ref, packed, field_out, even_out, diag_out, send):
    row = row_ref[0] % NY
    core = row_ref[0] // NY % NC

    def wide(which, columns):
        return reorder(
            jnp.concatenate([packed[which * NY + y][:, columns] for y in range(NY)], axis=1), row
        )

    field = wide(core, slice(0, H))
    field_out[...] = field
    even_out[...] = wide(1 - core, slice(0, H))
    diag_out[...] = wide(core, slice(H, 2 * H))
    store_parts(send, field, row)


def next_field(parts, blocks, field, previous, diag, beside, wait=None):
    sums = []
    for block in blocks[::-1]:
        if wait is not None and block is blocks[0]:
            wait()
        total = None
        for z in range(NZ):
            term = lax.dot_general(
                parts[z],
                block[:, z * W : (z + 1) * W],
                (((1,), (1,)), ((), ())),
                preferred_element_type=F32,
            )
            total = term if total is None else total + term
        sums.append(total if total.shape[0] == B else total[:B] + total[B:])
    blended = jnp.concatenate(sums[::-1], axis=1)
    own = (diag[0:1] + (2.0 - CENTRE)) * field[...]
    total = own + blended
    if previous is not None:
        total = total - LINK * previous[...]
    if beside is not None:
        total = total - beside
    return total * (1.0 / SCALE)


def first_step(row_ref, own, parts, c1, c2, c3, diag, up, down, field, field_out, send, c0, arrived):
    fetch = pltpu.make_async_copy(own, c0, arrived)
    fetch.start()
    beside = up[...] + down[...]
    out = next_field(parts, (c0, c1, c2, c3), field, None, diag, beside, fetch.wait)
    field_out[...] = out
    store_parts(send, out, row_ref[0] % NY)


def step(row_ref, parts, c0, c1, c2, c3, diag, up, down, field, previous, field_out, send):
    out = next_field(parts, (c0, c1, c2, c3), field, previous, diag, up[...] + down[...])
    field_out[...] = out
    store_parts(send, out, row_ref[0] % NY)


def last_step(parts, c0, c1, c2, c3, field, diag, f0, f1, f2, u0, d0, u1, d1, u2, d2, send):
    partial = next_field(parts, (c0, c1, c2, c3), field, f2, diag, None)
    f3 = field[...]
    fields = [f0[...], f1[...], f2[...], f3]
    beside = [u0[...] + d0[...], u1[...] + d1[...], u2[...] + d2[...]]
    lane = lax.broadcasted_iota(jnp.int32, (B, 128), 1)
    table = jnp.zeros((B, 128), F32)
    for p, (i, j) in enumerate(PAIRS):
        if j < STEPS:
            terms = fields[i] * fields[j]
        elif i < STEPS - 1:
            terms = partial * fields[i] - f3 * beside[i] * (1.0 / SCALE)
        else:
            continue
        table = jnp.where(lane == p, jnp.sum(terms, axis=1, keepdims=True), table)
    packed = jnp.concatenate([table, partial, f3], axis=1)
    for k in range(NX * NC):
        send[k] = packed


def add_up(plane_ref, packed, last_out, send):
    count = NX * NC
    inv = 1.0 / SCALE

    def partial(p):
        return packed[p][:, 128 : 128 + W]

    def before(p):
        return packed[p][:, 128 + W :]

    table = packed[0][:, :128]
    for p in range(1, count):
        table = table + packed[p][:, :128]
    square = cross = jnp.zeros((B, W), F32)
    for p in range(count):
        beside = before(p - 1) if p > 0 else 0.0
        if p + 1 < count:
            beside = beside + before(p + 1)
        last = partial(p) - beside * inv
        square = square + last * last
        cross = cross + last * before(p)
    lane = lax.broadcasted_iota(jnp.int32, (B, 128), 1)
    for pair, terms in (((STEPS - 1, STEPS), cross), ((STEPS, STEPS), square)):
        value = jnp.sum(terms, axis=1, keepdims=True)
        table = jnp.where(lane == PAIRS.index(pair), value, table)
    for z in range(NZ):
        send[z] = table
    plane = plane_ref[0] // NY
    above = jnp.where(plane > 0, before(jnp.maximum(plane - 1, 0)), 0.0)
    below = jnp.where(plane + 1 < count, before(jnp.minimum(plane + 1, count - 1)), 0.0)
    last_out[...] = partial(plane) - (above + below) * inv


def finish(tables, f0, f1, f2, f3, f4, solution_out, residual_out):
    total = tables[0]
    for z in range(1, NZ):
        total = total + tables[z]
    gram = {}
    for p, (i, j) in enumerate(PAIRS):
        gram[i, j] = gram[j, i] = total[:, p : p + 1]

    def inner(a, c):
        total = None
        for j, cj in enumerate(c):
            part = None
            for i, ai in enumerate(a):
                term = gram[i, j] if ai is None else ai * gram[i, j]
                part = term if part is None else part + term
            part = part if cj is None else part * cj
            total = part if total is None else total + part
        return total

    def plus(a, c, scale):
        out = []
        for k in range(max(len(a), len(c))):
            if k >= len(c):
                out.append(a[k])
            elif k >= len(a):
                out.append(scale * c[k])
            else:
                out.append(a[k] + scale * c[k])
        return out

    def image(a):
        out = [CENTRE * x for x in a] + [jnp.zeros_like(a[0])]
        for k, x in enumerate(a):
            out[k + 1] = out[k + 1] + SCALE * x
            if k > 0:
                out[k - 1] = out[k - 1] + LINK * x
        return out

    one = jnp.ones((B, 1), F32)
    source = [None]
    found = None
    residual = search = [one]
    rho = gram[0, 0]
    for iteration in range(2):
        image_one = image(search)
        alpha = rho / inner(source, image_one)
        interim = plus(residual, image_one, -alpha)
        image_two = image(interim)
        omega = inner(image_two, interim) / inner(image_two, image_two)
        if found is None:
            found = [alpha * x for x in search]
        else:
            found = plus(found, search, alpha)
        found = plus(found, interim, omega)
        residual = plus(interim, image_two, -omega)
        if iteration == 0:
            rho_next = inner(source, residual)
            beta = (rho_next / rho) * (alpha / omega)
            search = plus(residual, plus(search, image_one, -omega), beta)
            rho = rho_next
    fields = [f[:, :H] for f in (f0, f1, f2, f3, f4)]

    def combine(a):
        out = a[0] * fields[0]
        for k in range(1, len(a)):
            out = out + a[k] * fields[k]
        return out

    solution_out[...] = combine(found)
    residual_out[...] = combine(residual)


def swapped(array, mask):
    return lax.ppermute(array, "y", [(y, y ^ mask) for y in range(NY)])


def even(field):
    return lax.ppermute(field, ("x", "c"), [(i, i ^ 1) for i in range(NX * NC)])


def odd(field):
    pairs = [(i, i + 1) for i in range(1, NX * NC - 1, 2)]
    return lax.ppermute(field, ("x", "c"), pairs + [(j, i) for i, j in pairs])


def on_device(source, coupling, diagonal):
    own = coupling[0]
    row = lax.axis_index(("x", "c", "y")).astype(jnp.int32).reshape(1)
    packed = jnp.concatenate([source[0], jnp.broadcast_to(diagonal, (B, H))], axis=1)
    packed = jnp.broadcast_to(packed[None], (NC * NY, B, 128))
    packed = lax.all_to_all(packed, ("c", "y"), 0, 0, tiled=True)
    by_1, by_3 = swapped(own, 1), swapped(own, 3)
    by_1, packed = lax.optimization_barrier((by_1, packed))
    blocks = [own, by_1, swapped(by_1, 3), by_3]
    shape = jax.ShapeDtypeStruct
    wide = shape((B, W), F32)
    sends = [shape((NZ, 2 * B if low else B, W), BF16) for low in WITH_LOW]
    field, up, diag, send = call(unpack, (wide, wide, wide, sends[0]), row, packed, smem=1)
    fields, beside = [field], []
    for k in range(STEPS - 1):
        down = odd(field)
        if k > 0:
            up = even(field)
        beside += [up, down]
        parts = lax.all_to_all(send, "z", 0, 0, tiled=True)
        outs = (wide, sends[k + 1])
        if k == 0:
            field, send = call(
                first_step, outs, row, own, parts, *blocks[1:], diag, up, down, field,
                smem=1,
                hbm=1,
                scratch=[pltpu.VMEM((H, NZ * W), BF16), pltpu.SemaphoreType.DMA],
            )
            blocks[0], field = lax.optimization_barrier((own, field))
        else:
            field, send = call(
                step, outs, row, parts, *blocks, diag, up, down, *fields[::-1][:2], smem=1
            )
        fields.append(field)
    parts = lax.all_to_all(send, "z", 0, 0, tiled=True)
    packed = call(
        last_step,
        shape((NX * NC, B, 128 + 2 * W), F32),
        parts, *blocks, field, diag, *fields[:3], *beside,
    )
    packed = lax.all_to_all(packed, ("x", "c"), 0, 0, tiled=True)
    last, table = call(add_up, (wide, shape((NZ, B, 128), F32)), row, packed, smem=1)
    table = lax.all_to_all(table, "z", 0, 0, tiled=True)
    own_shape = shape((B, H), F32)
    found, residual = call(finish, (own_shape, own_shape), table, *fields, last, keep=False)
    return found[None], residual[None]


def solution(mesh):
    fine = Mesh(mesh.devices.reshape(NX, NC, NZ, NY), ("x", "c", "z", "y"))
    depth, harm = ("x", "c"), ("z", "y")
    return jax.shard_map(
        on_device,
        mesh=fine,
        in_specs=(P(depth, None, harm), P(depth, harm, None), P(depth, harm)),
        out_specs=(P(depth, None, harm), P(depth, None, harm)),
        check_vma=False,
    )
```

```python
import jax
import jax.numpy as jnp
from jax import lax
from jax.experimental import pallas as pl
from jax.experimental.pallas import tpu as pltpu
from jax.sharding import Mesh, PartitionSpec as P

STEPS = 4
CENTRE = 6.75
SCALE = 32.0
LINK = (6.5**2 / 12 + 2.0) / SCALE
WITH_LOW = (False, True, True, False)
PAIRS = [(i, j) for j in range(STEPS + 1) for i in range(j + 1)]
NZ, NY, NX, NC = 16, 4, 4, 2
B = 8
H = 64
W = NY * H
F32 = jnp.float32
BF16 = jnp.bfloat16


def call(body, outs, *args, smem=0, hbm=0, scratch=(), keep=True):
    first = smem + hbm
    args = args[:smem] + tuple(
        pltpu.with_memory_space_constraint(x, pltpu.VMEM if i >= hbm else pltpu.HBM)
        for i, x in enumerate(args[smem:])
    )
    if keep:
        outs = jax.tree.map(lambda o: pltpu.VMEM(o.shape, o.dtype), outs)
    places = [pltpu.SMEM] * smem + [pltpu.HBM] * hbm + [pltpu.VMEM] * (len(args) - first)
    specs = [pl.BlockSpec(memory_space=place) for place in places]
    return pl.pallas_call(
        body,
        out_shape=outs,
        in_specs=specs,
        scratch_shapes=scratch,
        compiler_params=pltpu.CompilerParams(vmem_limit_bytes=8 << 20),
        out_specs=jax.tree.map(lambda _: pl.BlockSpec(memory_space=pltpu.VMEM), outs),
    )(*args)


def reorder(field, row):
    lane = lax.broadcasted_iota(jnp.int32, field.shape, 1)
    pairs = jnp.where(lane % (2 * H) < H, pltpu.roll(field, W - H, 1), pltpu.roll(field, H, 1))
    field = jnp.where(row % 2 == 1, pairs, field)
    return jnp.where(row >= 2, pltpu.roll(field, 2 * H, 1), field)


def store_parts(send, field, row):
    turned = reorder(field, row)
    parts = turned.astype(BF16)
    if send.shape[1] > B:
        low = (turned - parts.astype(F32)).astype(BF16)
        parts = jnp.concatenate([parts, low], axis=0)
    for z in range(NZ):
        send[z] = parts


def unpack(row_ref, packed, field_out, even_out, diag_out, send):
    row = row_ref[0] % NY
    core = row_ref[0] // NY % NC

    def wide(which, columns):
        return reorder(
            jnp.concatenate([packed[which * NY + y][:, columns] for y in range(NY)], axis=1), row
        )

    field = wide(core, slice(0, H))
    field_out[...] = field
    even_out[...] = wide(1 - core, slice(0, H))
    diag_out[...] = wide(core, slice(H, 2 * H))
    store_parts(send, field, row)


def next_field(parts, blocks, field, previous, diag, beside, wait=None):
    sums = []
    for block in blocks[::-1]:
        if wait is not None and block is blocks[0]:
            wait()
        total = None
        for z in range(NZ):
            term = lax.dot_general(
                parts[z],
                block[:, z * W : (z + 1) * W],
                (((1,), (1,)), ((), ())),
                preferred_element_type=F32,
            )
            total = term if total is None else total + term
        sums.append(total if total.shape[0] == B else total[:B] + total[B:])
    blended = jnp.concatenate(sums[::-1], axis=1)
    own = (diag[0:1] + (2.0 - CENTRE)) * field[...]
    total = own + blended
    if previous is not None:
        total = total - LINK * previous[...]
    if beside is not None:
        total = total - beside
    return total * (1.0 / SCALE)


def first_step(row_ref, own, parts, c1, c2, c3, diag, up, down, field, field_out, send, c0, arrived):
    fetch = pltpu.make_async_copy(own, c0, arrived)
    fetch.start()
    beside = up[...] + down[...]
    out = next_field(parts, (c0, c1, c2, c3), field, None, diag, beside, fetch.wait)
    field_out[...] = out
    store_parts(send, out, row_ref[0] % NY)


def step(row_ref, parts, c0, c1, c2, c3, diag, up, down, field, previous, field_out, send):
    out = next_field(parts, (c0, c1, c2, c3), field, previous, diag, up[...] + down[...])
    field_out[...] = out
    store_parts(send, out, row_ref[0] % NY)


def last_step(parts, c0, c1, c2, c3, field, diag, f0, f1, f2, u0, d0, u1, d1, u2, d2, send):
    partial = next_field(parts, (c0, c1, c2, c3), field, f2, diag, None)
    f3 = field[...]
    fields = [f0[...], f1[...], f2[...], f3]
    beside = [u0[...] + d0[...], u1[...] + d1[...], u2[...] + d2[...]]
    lane = lax.broadcasted_iota(jnp.int32, (B, 128), 1)
    table = jnp.zeros((B, 128), F32)
    for p, (i, j) in enumerate(PAIRS):
        if j < STEPS:
            terms = fields[i] * fields[j]
        elif i < STEPS - 1:
            terms = partial * fields[i] - f3 * beside[i] * (1.0 / SCALE)
        else:
            continue
        table = jnp.where(lane == p, jnp.sum(terms, axis=1, keepdims=True), table)
    packed = jnp.concatenate([table, partial, f3], axis=1)
    for k in range(NX * NC):
        send[k] = packed


def add_up(plane_ref, packed, last_out, send):
    count = NX * NC
    inv = 1.0 / SCALE

    def partial(p):
        return packed[p][:, 128 : 128 + W]

    def before(p):
        return packed[p][:, 128 + W :]

    table = packed[0][:, :128]
    for p in range(1, count):
        table = table + packed[p][:, :128]
    square = cross = jnp.zeros((B, W), F32)
    for p in range(count):
        beside = before(p - 1) if p > 0 else 0.0
        if p + 1 < count:
            beside = beside + before(p + 1)
        last = partial(p) - beside * inv
        square = square + last * last
        cross = cross + last * before(p)
    lane = lax.broadcasted_iota(jnp.int32, (B, 128), 1)
    for pair, terms in (((STEPS - 1, STEPS), cross), ((STEPS, STEPS), square)):
        value = jnp.sum(terms, axis=1, keepdims=True)
        table = jnp.where(lane == PAIRS.index(pair), value, table)
    for z in range(NZ):
        send[z] = table
    plane = plane_ref[0] // NY
    above = jnp.where(plane > 0, before(jnp.maximum(plane - 1, 0)), 0.0)
    below = jnp.where(plane + 1 < count, before(jnp.minimum(plane + 1, count - 1)), 0.0)
    last_out[...] = partial(plane) - (above + below) * inv


def finish(tables, f0, f1, f2, f3, f4, solution_out, residual_out):
    total = tables[0]
    for z in range(1, NZ):
        total = total + tables[z]
    gram = {}
    for p, (i, j) in enumerate(PAIRS):
        gram[i, j] = gram[j, i] = total[:, p : p + 1]

    def inner(a, c):
        total = None
        for j, cj in enumerate(c):
            part = None
            for i, ai in enumerate(a):
                term = gram[i, j] if ai is None else ai * gram[i, j]
                part = term if part is None else part + term
            part = part if cj is None else part * cj
            total = part if total is None else total + part
        return total

    def plus(a, c, scale):
        out = []
        for k in range(max(len(a), len(c))):
            if k >= len(c):
                out.append(a[k])
            elif k >= len(a):
                out.append(scale * c[k])
            else:
                out.append(a[k] + scale * c[k])
        return out

    def image(a):
        out = [CENTRE * x for x in a] + [jnp.zeros_like(a[0])]
        for k, x in enumerate(a):
            out[k + 1] = out[k + 1] + SCALE * x
            if k > 0:
                out[k - 1] = out[k - 1] + LINK * x
        return out

    one = jnp.ones((B, 1), F32)
    source = [None]
    found = None
    residual = search = [one]
    rho = gram[0, 0]
    for iteration in range(2):
        image_one = image(search)
        alpha = rho / inner(source, image_one)
        interim = plus(residual, image_one, -alpha)
        image_two = image(interim)
        omega = inner(image_two, interim) / inner(image_two, image_two)
        if found is None:
            found = [alpha * x for x in search]
        else:
            found = plus(found, search, alpha)
        found = plus(found, interim, omega)
        residual = plus(interim, image_two, -omega)
        if iteration == 0:
            rho_next = inner(source, residual)
            beta = (rho_next / rho) * (alpha / omega)
            search = plus(residual, plus(search, image_one, -omega), beta)
            rho = rho_next
    fields = [f[:, :H] for f in (f0, f1, f2, f3, f4)]

    def combine(a):
        out = a[0] * fields[0]
        for k in range(1, len(a)):
            out = out + a[k] * fields[k]
        return out

    solution_out[...] = combine(found)
    residual_out[...] = combine(residual)


def swapped(array, mask):
    return lax.ppermute(array, "y", [(y, y ^ mask) for y in range(NY)])


def even(field):
    return lax.ppermute(field, ("x", "c"), [(i, i ^ 1) for i in range(NX * NC)])


def odd(field):
    pairs = [(i, i + 1) for i in range(1, NX * NC - 1, 2)]
    return lax.ppermute(field, ("x", "c"), pairs + [(j, i) for i, j in pairs])


def on_device(source, coupling, diagonal):
    own = coupling[0]
    row = lax.axis_index(("x", "c", "y")).astype(jnp.int32).reshape(1)
    packed = jnp.concatenate([source[0], jnp.broadcast_to(diagonal, (B, H))], axis=1)
    packed = jnp.broadcast_to(packed[None], (NC * NY, B, 128))
    packed = lax.all_to_all(packed, ("c", "y"), 0, 0, tiled=True)
    by_1, by_3 = swapped(own, 1), swapped(own, 3)
    by_1, packed = lax.optimization_barrier((by_1, packed))
    blocks = [own, by_1, swapped(by_1, 3), by_3]
    shape = jax.ShapeDtypeStruct
    wide = shape((B, W), F32)
    sends = [shape((NZ, 2 * B if low else B, W), BF16) for low in WITH_LOW]
    field, up, diag, send = call(unpack, (wide, wide, wide, sends[0]), row, packed, smem=1)
    fields, beside = [field], []
    for k in range(STEPS - 1):
        down = odd(field)
        if k > 0:
            up = even(field)
        beside += [up, down]
        parts = lax.all_to_all(send, "z", 0, 0, tiled=True)
        outs = (wide, sends[k + 1])
        if k == 0:
            field, send, blocks[0] = call(
                first_step, (*outs, shape((H, NZ * W), BF16)), row, own, parts, *blocks[1:], diag, up, down, field,
                smem=1,
                hbm=1,
                scratch=[pltpu.SemaphoreType.DMA],
            )
        else:
            field, send = call(
                step, outs, row, parts, *blocks, diag, up, down, *fields[::-1][:2], smem=1
            )
        fields.append(field)
    parts = lax.all_to_all(send, "z", 0, 0, tiled=True)
    packed = call(
        last_step,
        shape((NX * NC, B, 128 + 2 * W), F32),
        parts, *blocks, field, diag, *fields[:3], *beside,
    )
    packed = lax.all_to_all(packed, ("x", "c"), 0, 0, tiled=True)
    last, table = call(add_up, (wide, shape((NZ, B, 128), F32)), row, packed, smem=1)
    table = lax.all_to_all(table, "z", 0, 0, tiled=True)
    own_shape = shape((B, H), F32)
    found, residual = call(finish, (own_shape, own_shape), table, *fields, last, keep=False)
    return found[None], residual[None]


def solution(mesh):
    fine = Mesh(mesh.devices.reshape(NX, NC, NZ, NY), ("x", "c", "z", "y"))
    depth, harm = ("x", "c"), ("z", "y")
    return jax.shard_map(
        on_device,
        mesh=fine,
        in_specs=(P(depth, None, harm), P(depth, harm, None), P(depth, harm)),
        out_specs=(P(depth, None, harm), P(depth, None, harm)),
        check_vma=False,
    )
```

```python
import jax
import jax.numpy as jnp
from jax import lax
from jax.experimental import pallas as pl
from jax.experimental.pallas import tpu as pltpu
from jax.sharding import Mesh, PartitionSpec as P

STEPS = 4
CENTRE = 6.75
SCALE = 32.0
LINK = (6.5**2 / 12 + 2.0) / SCALE
WITH_LOW = (False, True, True, False)
PAIRS = [(i, j) for j in range(STEPS + 1) for i in range(j + 1)]
NZ, NY, NX, NC = 16, 4, 4, 2
B = 8
H = 64
FETCHES = 8
W = NY * H
F32 = jnp.float32
BF16 = jnp.bfloat16


def call(body, outs, *args, smem=0, hbm=0, scratch=(), keep=True):
    first = smem + hbm
    args = args[:smem] + tuple(
        pltpu.with_memory_space_constraint(x, pltpu.VMEM if i >= hbm else pltpu.HBM)
        for i, x in enumerate(args[smem:])
    )
    if keep:
        outs = jax.tree.map(lambda o: pltpu.VMEM(o.shape, o.dtype), outs)
    places = [pltpu.SMEM] * smem + [pltpu.HBM] * hbm + [pltpu.VMEM] * (len(args) - first)
    specs = [pl.BlockSpec(memory_space=place) for place in places]
    return pl.pallas_call(
        body,
        out_shape=outs,
        in_specs=specs,
        scratch_shapes=scratch,
        compiler_params=pltpu.CompilerParams(vmem_limit_bytes=8 << 20),
        out_specs=jax.tree.map(lambda _: pl.BlockSpec(memory_space=pltpu.VMEM), outs),
    )(*args)


def reorder(field, row):
    lane = lax.broadcasted_iota(jnp.int32, field.shape, 1)
    pairs = jnp.where(lane % (2 * H) < H, pltpu.roll(field, W - H, 1), pltpu.roll(field, H, 1))
    field = jnp.where(row % 2 == 1, pairs, field)
    return jnp.where(row >= 2, pltpu.roll(field, 2 * H, 1), field)


def store_parts(send, field, row):
    turned = reorder(field, row)
    parts = turned.astype(BF16)
    if send.shape[1] > B:
        low = (turned - parts.astype(F32)).astype(BF16)
        parts = jnp.concatenate([parts, low], axis=0)
    for z in range(NZ):
        send[z] = parts


def unpack(row_ref, packed, field_out, even_out, diag_out, send):
    row = row_ref[0] % NY
    core = row_ref[0] // NY % NC

    def wide(which, columns):
        return reorder(
            jnp.concatenate([packed[which * NY + y][:, columns] for y in range(NY)], axis=1), row
        )

    field = wide(core, slice(0, H))
    field_out[...] = field
    even_out[...] = wide(1 - core, slice(0, H))
    diag_out[...] = wide(core, slice(H, 2 * H))
    store_parts(send, field, row)


def next_field(parts, blocks, field, previous, diag, beside, wait=None):
    sums = []
    for block in blocks[::-1]:
        if wait is not None and block is blocks[0]:
            wait()
        total = None
        for z in range(NZ):
            term = lax.dot_general(
                parts[z],
                block[:, z * W : (z + 1) * W],
                (((1,), (1,)), ((), ())),
                preferred_element_type=F32,
            )
            total = term if total is None else total + term
        sums.append(total if total.shape[0] == B else total[:B] + total[B:])
    blended = jnp.concatenate(sums[::-1], axis=1)
    own = (diag[0:1] + (2.0 - CENTRE)) * field[...]
    total = own + blended
    if previous is not None:
        total = total - LINK * previous[...]
    if beside is not None:
        total = total - beside
    return total * (1.0 / SCALE)


def first_step(row_ref, own, parts, c1, c2, c3, diag, up, down, field, field_out, send, c0, arrived):
    rows = [pl.ds(k * H // FETCHES, H // FETCHES) for k in range(FETCHES)]
    fetches = [
        pltpu.make_async_copy(own.at[part], c0.at[part], arrived.at[k])
        for k, part in enumerate(rows)
    ]
    for fetch in fetches:
        fetch.start()

    def wait():
        for fetch in fetches:
            fetch.wait()

    beside = up[...] + down[...]
    out = next_field(parts, (c0, c1, c2, c3), field, None, diag, beside, wait)
    field_out[...] = out
    store_parts(send, out, row_ref[0] % NY)


def step(row_ref, parts, c0, c1, c2, c3, diag, up, down, field, previous, field_out, send):
    out = next_field(parts, (c0, c1, c2, c3), field, previous, diag, up[...] + down[...])
    field_out[...] = out
    store_parts(send, out, row_ref[0] % NY)


def last_step(parts, c0, c1, c2, c3, field, diag, f0, f1, f2, u0, d0, u1, d1, u2, d2, send):
    partial = next_field(parts, (c0, c1, c2, c3), field, f2, diag, None)
    f3 = field[...]
    fields = [f0[...], f1[...], f2[...], f3]
    beside = [u0[...] + d0[...], u1[...] + d1[...], u2[...] + d2[...]]
    lane = lax.broadcasted_iota(jnp.int32, (B, 128), 1)
    table = jnp.zeros((B, 128), F32)
    for p, (i, j) in enumerate(PAIRS):
        if j < STEPS:
            terms = fields[i] * fields[j]
        elif i < STEPS - 1:
            terms = partial * fields[i] - f3 * beside[i] * (1.0 / SCALE)
        else:
            continue
        table = jnp.where(lane == p, jnp.sum(terms, axis=1, keepdims=True), table)
    packed = jnp.concatenate([table, partial, f3], axis=1)
    for k in range(NX * NC):
        send[k] = packed


def add_up(plane_ref, packed, last_out, send):
    count = NX * NC
    inv = 1.0 / SCALE

    def partial(p):
        return packed[p][:, 128 : 128 + W]

    def before(p):
        return packed[p][:, 128 + W :]

    table = packed[0][:, :128]
    for p in range(1, count):
        table = table + packed[p][:, :128]
    square = cross = jnp.zeros((B, W), F32)
    for p in range(count):
        beside = before(p - 1) if p > 0 else 0.0
        if p + 1 < count:
            beside = beside + before(p + 1)
        last = partial(p) - beside * inv
        square = square + last * last
        cross = cross + last * before(p)
    lane = lax.broadcasted_iota(jnp.int32, (B, 128), 1)
    for pair, terms in (((STEPS - 1, STEPS), cross), ((STEPS, STEPS), square)):
        value = jnp.sum(terms, axis=1, keepdims=True)
        table = jnp.where(lane == PAIRS.index(pair), value, table)
    for z in range(NZ):
        send[z] = table
    plane = plane_ref[0] // NY
    above = jnp.where(plane > 0, before(jnp.maximum(plane - 1, 0)), 0.0)
    below = jnp.where(plane + 1 < count, before(jnp.minimum(plane + 1, count - 1)), 0.0)
    last_out[...] = partial(plane) - (above + below) * inv


def finish(tables, f0, f1, f2, f3, f4, solution_out, residual_out):
    total = tables[0]
    for z in range(1, NZ):
        total = total + tables[z]
    gram = {}
    for p, (i, j) in enumerate(PAIRS):
        gram[i, j] = gram[j, i] = total[:, p : p + 1]

    def inner(a, c):
        total = None
        for j, cj in enumerate(c):
            part = None
            for i, ai in enumerate(a):
                term = gram[i, j] if ai is None else ai * gram[i, j]
                part = term if part is None else part + term
            part = part if cj is None else part * cj
            total = part if total is None else total + part
        return total

    def plus(a, c, scale):
        out = []
        for k in range(max(len(a), len(c))):
            if k >= len(c):
                out.append(a[k])
            elif k >= len(a):
                out.append(scale * c[k])
            else:
                out.append(a[k] + scale * c[k])
        return out

    def image(a):
        out = [CENTRE * x for x in a] + [jnp.zeros_like(a[0])]
        for k, x in enumerate(a):
            out[k + 1] = out[k + 1] + SCALE * x
            if k > 0:
                out[k - 1] = out[k - 1] + LINK * x
        return out

    one = jnp.ones((B, 1), F32)
    source = [None]
    found = None
    residual = search = [one]
    rho = gram[0, 0]
    for iteration in range(2):
        image_one = image(search)
        alpha = rho / inner(source, image_one)
        interim = plus(residual, image_one, -alpha)
        image_two = image(interim)
        omega = inner(image_two, interim) / inner(image_two, image_two)
        if found is None:
            found = [alpha * x for x in search]
        else:
            found = plus(found, search, alpha)
        found = plus(found, interim, omega)
        residual = plus(interim, image_two, -omega)
        if iteration == 0:
            rho_next = inner(source, residual)
            beta = (rho_next / rho) * (alpha / omega)
            search = plus(residual, plus(search, image_one, -omega), beta)
            rho = rho_next
    fields = [f[:, :H] for f in (f0, f1, f2, f3, f4)]

    def combine(a):
        out = a[0] * fields[0]
        for k in range(1, len(a)):
            out = out + a[k] * fields[k]
        return out

    solution_out[...] = combine(found)
    residual_out[...] = combine(residual)


def swapped(array, mask):
    return lax.ppermute(array, "y", [(y, y ^ mask) for y in range(NY)])


def even(field):
    return lax.ppermute(field, ("x", "c"), [(i, i ^ 1) for i in range(NX * NC)])


def odd(field):
    pairs = [(i, i + 1) for i in range(1, NX * NC - 1, 2)]
    return lax.ppermute(field, ("x", "c"), pairs + [(j, i) for i, j in pairs])


def on_device(source, coupling, diagonal):
    own = coupling[0]
    row = lax.axis_index(("x", "c", "y")).astype(jnp.int32).reshape(1)
    packed = jnp.concatenate([source[0], jnp.broadcast_to(diagonal, (B, H))], axis=1)
    packed = jnp.broadcast_to(packed[None], (NC * NY, B, 128))
    packed = lax.all_to_all(packed, ("c", "y"), 0, 0, tiled=True)
    by_1, by_3 = swapped(own, 1), swapped(own, 3)
    by_1, packed = lax.optimization_barrier((by_1, packed))
    blocks = [own, by_1, swapped(by_1, 3), by_3]
    shape = jax.ShapeDtypeStruct
    wide = shape((B, W), F32)
    sends = [shape((NZ, 2 * B if low else B, W), BF16) for low in WITH_LOW]
    field, up, diag, send = call(unpack, (wide, wide, wide, sends[0]), row, packed, smem=1)
    fields, beside = [field], []
    for k in range(STEPS - 1):
        down = odd(field)
        if k > 0:
            up = even(field)
        beside += [up, down]
        parts = lax.all_to_all(send, "z", 0, 0, tiled=True)
        outs = (wide, sends[k + 1])
        if k == 0:
            field, send, blocks[0] = call(
                first_step, (*outs, shape((H, NZ * W), BF16)), row, own, parts, *blocks[1:], diag, up, down, field,
                smem=1,
                hbm=1,
                scratch=[pltpu.SemaphoreType.DMA((FETCHES,))],
            )
        else:
            field, send = call(
                step, outs, row, parts, *blocks, diag, up, down, *fields[::-1][:2], smem=1
            )
        fields.append(field)
    parts = lax.all_to_all(send, "z", 0, 0, tiled=True)
    packed = call(
        last_step,
        shape((NX * NC, B, 128 + 2 * W), F32),
        parts, *blocks, field, diag, *fields[:3], *beside,
    )
    packed = lax.all_to_all(packed, ("x", "c"), 0, 0, tiled=True)
    last, table = call(add_up, (wide, shape((NZ, B, 128), F32)), row, packed, smem=1)
    table = lax.all_to_all(table, "z", 0, 0, tiled=True)
    own_shape = shape((B, H), F32)
    found, residual = call(finish, (own_shape, own_shape), table, *fields, last, keep=False)
    return found[None], residual[None]


def solution(mesh):
    fine = Mesh(mesh.devices.reshape(NX, NC, NZ, NY), ("x", "c", "z", "y"))
    depth, harm = ("x", "c"), ("z", "y")
    return jax.shard_map(
        on_device,
        mesh=fine,
        in_specs=(P(depth, None, harm), P(depth, harm, None), P(depth, harm)),
        out_specs=(P(depth, None, harm), P(depth, None, harm)),
        check_vma=False,
    )
```

```python
import jax
import jax.numpy as jnp
from jax import lax
from jax.experimental import pallas as pl
from jax.experimental.pallas import tpu as pltpu
from jax.sharding import Mesh, PartitionSpec as P

STEPS = 4
CENTRE = 6.75
SCALE = 32.0
LINK = (6.5**2 / 12 + 2.0) / SCALE
WITH_LOW = (False, True, True, False)
PAIRS = [(i, j) for j in range(STEPS + 1) for i in range(j + 1)]
NZ, NY, NX, NC = 16, 4, 4, 2
B = 8
H = 64
W = NY * H
F32 = jnp.float32
BF16 = jnp.bfloat16


def call(body, outs, *args, smem=0, hbm=0, scratch=(), keep=True):
    first = smem + hbm
    args = args[:smem] + tuple(
        pltpu.with_memory_space_constraint(x, pltpu.VMEM if i >= hbm else pltpu.HBM)
        for i, x in enumerate(args[smem:])
    )
    if keep:
        outs = jax.tree.map(lambda o: pltpu.VMEM(o.shape, o.dtype), outs)
    places = [pltpu.SMEM] * smem + [pltpu.HBM] * hbm + [pltpu.VMEM] * (len(args) - first)
    specs = [pl.BlockSpec(memory_space=place) for place in places]
    return pl.pallas_call(
        body,
        out_shape=outs,
        in_specs=specs,
        scratch_shapes=scratch,
        compiler_params=pltpu.CompilerParams(vmem_limit_bytes=8 << 20),
        out_specs=jax.tree.map(lambda _: pl.BlockSpec(memory_space=pltpu.VMEM), outs),
    )(*args)


def reorder(field, row):
    lane = lax.broadcasted_iota(jnp.int32, field.shape, 1)
    pairs = jnp.where(lane % (2 * H) < H, pltpu.roll(field, W - H, 1), pltpu.roll(field, H, 1))
    field = jnp.where(row % 2 == 1, pairs, field)
    return jnp.where(row >= 2, pltpu.roll(field, 2 * H, 1), field)


def store_parts(send, field, row):
    turned = reorder(field, row)
    parts = turned.astype(BF16)
    if send.shape[1] > B:
        low = (turned - parts.astype(F32)).astype(BF16)
        parts = jnp.concatenate([parts, low], axis=0)
    for z in range(NZ):
        send[z] = parts


def unpack(row_ref, packed, field_out, up_out, down_out, diag_out, send):
    row = row_ref[0] % NY
    plane = row_ref[0] // NY
    top = NX * NC - 1

    def wide(which, columns):
        return reorder(
            jnp.concatenate([packed[which * NY + y][:, columns] for y in range(NY)], axis=1), row
        )

    field = wide(plane, slice(0, H))
    field_out[...] = field
    up_out[...] = jnp.where(plane > 0, wide(jnp.maximum(plane - 1, 0), slice(0, H)), 0.0)
    down_out[...] = jnp.where(plane < top, wide(jnp.minimum(plane + 1, top), slice(0, H)), 0.0)
    diag_out[...] = wide(plane, slice(H, 2 * H))
    store_parts(send, field, row)


def next_field(parts, blocks, field, previous, diag, beside, wait=None):
    sums = []
    for block in blocks[::-1]:
        if wait is not None and block is blocks[0]:
            wait()
        total = None
        for z in range(NZ):
            term = lax.dot_general(
                parts[z],
                block[:, z * W : (z + 1) * W],
                (((1,), (1,)), ((), ())),
                preferred_element_type=F32,
            )
            total = term if total is None else total + term
        sums.append(total if total.shape[0] == B else total[:B] + total[B:])
    blended = jnp.concatenate(sums[::-1], axis=1)
    own = (diag[0:1] + (2.0 - CENTRE)) * field[...]
    total = own + blended
    if previous is not None:
        total = total - LINK * previous[...]
    if beside is not None:
        total = total - beside
    return total * (1.0 / SCALE)


def first_step(row_ref, own, parts, c1, c2, c3, diag, up, down, field, field_out, send, c0, arrived):
    fetch = pltpu.make_async_copy(own, c0, arrived)
    fetch.start()
    beside = up[...] + down[...]
    out = next_field(parts, (c0, c1, c2, c3), field, None, diag, beside, fetch.wait)
    field_out[...] = out
    store_parts(send, out, row_ref[0] % NY)


def step(row_ref, parts, c0, c1, c2, c3, diag, up, down, field, previous, field_out, send):
    out = next_field(parts, (c0, c1, c2, c3), field, previous, diag, up[...] + down[...])
    field_out[...] = out
    store_parts(send, out, row_ref[0] % NY)


def last_step(parts, c0, c1, c2, c3, field, diag, f0, f1, f2, u0, d0, u1, d1, u2, d2, send):
    partial = next_field(parts, (c0, c1, c2, c3), field, f2, diag, None)
    f3 = field[...]
    fields = [f0[...], f1[...], f2[...], f3]
    beside = [u0[...] + d0[...], u1[...] + d1[...], u2[...] + d2[...]]
    lane = lax.broadcasted_iota(jnp.int32, (B, 128), 1)
    table = jnp.zeros((B, 128), F32)
    for p, (i, j) in enumerate(PAIRS):
        if j < STEPS:
            terms = fields[i] * fields[j]
        elif i < STEPS - 1:
            terms = partial * fields[i] - f3 * beside[i] * (1.0 / SCALE)
        else:
            continue
        table = jnp.where(lane == p, jnp.sum(terms, axis=1, keepdims=True), table)
    packed = jnp.concatenate([table, partial, f3], axis=1)
    for k in range(NX * NC):
        send[k] = packed


def add_up(plane_ref, packed, last_out, send):
    count = NX * NC
    inv = 1.0 / SCALE

    def partial(p):
        return packed[p][:, 128 : 128 + W]

    def before(p):
        return packed[p][:, 128 + W :]

    table = packed[0][:, :128]
    for p in range(1, count):
        table = table + packed[p][:, :128]
    square = cross = jnp.zeros((B, W), F32)
    for p in range(count):
        beside = before(p - 1) if p > 0 else 0.0
        if p + 1 < count:
            beside = beside + before(p + 1)
        last = partial(p) - beside * inv
        square = square + last * last
        cross = cross + last * before(p)
    lane = lax.broadcasted_iota(jnp.int32, (B, 128), 1)
    for pair, terms in (((STEPS - 1, STEPS), cross), ((STEPS, STEPS), square)):
        value = jnp.sum(terms, axis=1, keepdims=True)
        table = jnp.where(lane == PAIRS.index(pair), value, table)
    for z in range(NZ):
        send[z] = table
    plane = plane_ref[0] // NY
    above = jnp.where(plane > 0, before(jnp.maximum(plane - 1, 0)), 0.0)
    below = jnp.where(plane + 1 < count, before(jnp.minimum(plane + 1, count - 1)), 0.0)
    last_out[...] = partial(plane) - (above + below) * inv


def finish(tables, f0, f1, f2, f3, f4, solution_out, residual_out):
    total = tables[0]
    for z in range(1, NZ):
        total = total + tables[z]
    gram = {}
    for p, (i, j) in enumerate(PAIRS):
        gram[i, j] = gram[j, i] = total[:, p : p + 1]

    def inner(a, c):
        total = None
        for j, cj in enumerate(c):
            part = None
            for i, ai in enumerate(a):
                term = gram[i, j] if ai is None else ai * gram[i, j]
                part = term if part is None else part + term
            part = part if cj is None else part * cj
            total = part if total is None else total + part
        return total

    def plus(a, c, scale):
        out = []
        for k in range(max(len(a), len(c))):
            if k >= len(c):
                out.append(a[k])
            elif k >= len(a):
                out.append(scale * c[k])
            else:
                out.append(a[k] + scale * c[k])
        return out

    def image(a):
        out = [CENTRE * x for x in a] + [jnp.zeros_like(a[0])]
        for k, x in enumerate(a):
            out[k + 1] = out[k + 1] + SCALE * x
            if k > 0:
                out[k - 1] = out[k - 1] + LINK * x
        return out

    one = jnp.ones((B, 1), F32)
    source = [None]
    found = None
    residual = search = [one]
    rho = gram[0, 0]
    for iteration in range(2):
        image_one = image(search)
        alpha = rho / inner(source, image_one)
        interim = plus(residual, image_one, -alpha)
        image_two = image(interim)
        omega = inner(image_two, interim) / inner(image_two, image_two)
        if found is None:
            found = [alpha * x for x in search]
        else:
            found = plus(found, search, alpha)
        found = plus(found, interim, omega)
        residual = plus(interim, image_two, -omega)
        if iteration == 0:
            rho_next = inner(source, residual)
            beta = (rho_next / rho) * (alpha / omega)
            search = plus(residual, plus(search, image_one, -omega), beta)
            rho = rho_next
    fields = [f[:, :H] for f in (f0, f1, f2, f3, f4)]

    def combine(a):
        out = a[0] * fields[0]
        for k in range(1, len(a)):
            out = out + a[k] * fields[k]
        return out

    solution_out[...] = combine(found)
    residual_out[...] = combine(residual)


def swapped(array, mask):
    return lax.ppermute(array, "y", [(y, y ^ mask) for y in range(NY)])


def even(field):
    return lax.ppermute(field, ("x", "c"), [(i, i ^ 1) for i in range(NX * NC)])


def odd(field):
    pairs = [(i, i + 1) for i in range(1, NX * NC - 1, 2)]
    return lax.ppermute(field, ("x", "c"), pairs + [(j, i) for i, j in pairs])


def on_device(source, coupling, diagonal):
    own = coupling[0]
    row = lax.axis_index(("x", "c", "y")).astype(jnp.int32).reshape(1)
    packed = jnp.concatenate([source[0], jnp.broadcast_to(diagonal, (B, H))], axis=1)
    packed = jnp.broadcast_to(packed[None], (NX * NC * NY, B, 128))
    packed = lax.all_to_all(packed, ("x", "c", "y"), 0, 0, tiled=True)
    by_1, by_3 = swapped(own, 1), swapped(own, 3)
    by_1, packed = lax.optimization_barrier((by_1, packed))
    blocks = [own, by_1, swapped(by_1, 3), by_3]
    shape = jax.ShapeDtypeStruct
    wide = shape((B, W), F32)
    sends = [shape((NZ, 2 * B if low else B, W), BF16) for low in WITH_LOW]
    field, up, down, diag, send = call(
        unpack, (wide, wide, wide, wide, sends[0]), row, packed, smem=1
    )
    fields, beside = [field], []
    for k in range(STEPS - 1):
        if k > 0:
            up, down = even(field), odd(field)
        beside += [up, down]
        parts = lax.all_to_all(send, "z", 0, 0, tiled=True)
        outs = (wide, sends[k + 1])
        if k == 0:
            field, send, blocks[0] = call(
                first_step, (*outs, shape((H, NZ * W), BF16)), row, own, parts, *blocks[1:], diag, up, down, field,
                smem=1,
                hbm=1,
                scratch=[pltpu.SemaphoreType.DMA],
            )
        else:
            field, send = call(
                step, outs, row, parts, *blocks, diag, up, down, *fields[::-1][:2], smem=1
            )
        fields.append(field)
    parts = lax.all_to_all(send, "z", 0, 0, tiled=True)
    packed = call(
        last_step,
        shape((NX * NC, B, 128 + 2 * W), F32),
        parts, *blocks, field, diag, *fields[:3], *beside,
    )
    packed = lax.all_to_all(packed, ("x", "c"), 0, 0, tiled=True)
    last, table = call(add_up, (wide, shape((NZ, B, 128), F32)), row, packed, smem=1)
    table = lax.all_to_all(table, "z", 0, 0, tiled=True)
    own_shape = shape((B, H), F32)
    found, residual = call(finish, (own_shape, own_shape), table, *fields, last, keep=False)
    return found[None], residual[None]


def solution(mesh):
    fine = Mesh(mesh.devices.reshape(NX, NC, NZ, NY), ("x", "c", "z", "y"))
    depth, harm = ("x", "c"), ("z", "y")
    return jax.shard_map(
        on_device,
        mesh=fine,
        in_specs=(P(depth, None, harm), P(depth, harm, None), P(depth, harm)),
        out_specs=(P(depth, None, harm), P(depth, None, harm)),
        check_vma=False,
    )
```

```python
import jax
import jax.numpy as jnp
from jax import lax
from jax.experimental import pallas as pl
from jax.experimental.pallas import tpu as pltpu
from jax.sharding import Mesh, PartitionSpec as P

STEPS = 4
CENTRE = 6.75
SCALE = 32.0
LINK = (6.5**2 / 12 + 2.0) / SCALE
WITH_LOW = (False, True, False, False)
PAIRS = [(i, j) for j in range(STEPS + 1) for i in range(j + 1)]
NZ, NY, NX, NC = 16, 4, 4, 2
B = 8
H = 64
W = NY * H
F32 = jnp.float32
BF16 = jnp.bfloat16


def call(body, outs, *args, smem=0, hbm=0, scratch=(), keep=True):
    first = smem + hbm
    args = args[:smem] + tuple(
        pltpu.with_memory_space_constraint(x, pltpu.VMEM if i >= hbm else pltpu.HBM)
        for i, x in enumerate(args[smem:])
    )
    if keep:
        outs = jax.tree.map(lambda o: pltpu.VMEM(o.shape, o.dtype), outs)
    places = [pltpu.SMEM] * smem + [pltpu.HBM] * hbm + [pltpu.VMEM] * (len(args) - first)
    specs = [pl.BlockSpec(memory_space=place) for place in places]
    return pl.pallas_call(
        body,
        out_shape=outs,
        in_specs=specs,
        scratch_shapes=scratch,
        compiler_params=pltpu.CompilerParams(vmem_limit_bytes=8 << 20),
        out_specs=jax.tree.map(lambda _: pl.BlockSpec(memory_space=pltpu.VMEM), outs),
    )(*args)


def reorder(field, row):
    lane = lax.broadcasted_iota(jnp.int32, field.shape, 1)
    pairs = jnp.where(lane % (2 * H) < H, pltpu.roll(field, W - H, 1), pltpu.roll(field, H, 1))
    field = jnp.where(row % 2 == 1, pairs, field)
    return jnp.where(row >= 2, pltpu.roll(field, 2 * H, 1), field)


def store_parts(send, field, row):
    turned = reorder(field, row)
    parts = turned.astype(BF16)
    if send.shape[1] > B:
        low = (turned - parts.astype(F32)).astype(BF16)
        parts = jnp.concatenate([parts, low], axis=0)
    for z in range(NZ):
        send[z] = parts


def unpack(row_ref, packed, field_out, even_out, diag_out, send):
    row = row_ref[0] % NY
    core = row_ref[0] // NY % NC

    def wide(which, columns):
        return reorder(
            jnp.concatenate([packed[which * NY + y][:, columns] for y in range(NY)], axis=1), row
        )

    field = wide(core, slice(0, H))
    field_out[...] = field
    even_out[...] = wide(1 - core, slice(0, H))
    diag_out[...] = wide(core, slice(H, 2 * H))
    store_parts(send, field, row)


def next_field(parts, blocks, field, previous, diag, beside, wait=None):
    sums = []
    for block in blocks[::-1]:
        if wait is not None and block is blocks[0]:
            wait()
        total = None
        for z in range(NZ):
            term = lax.dot_general(
                parts[z],
                block[:, z * W : (z + 1) * W],
                (((1,), (1,)), ((), ())),
                preferred_element_type=F32,
            )
            total = term if total is None else total + term
        sums.append(total if total.shape[0] == B else total[:B] + total[B:])
    blended = jnp.concatenate(sums[::-1], axis=1)
    own = (diag[0:1] + (2.0 - CENTRE)) * field[...]
    total = own + blended
    if previous is not None:
        total = total - LINK * previous[...]
    if beside is not None:
        total = total - beside
    return total * (1.0 / SCALE)


def first_step(row_ref, own, parts, c1, c2, c3, diag, up, down, field, field_out, send, c0, arrived):
    fetch = pltpu.make_async_copy(own, c0, arrived)
    fetch.start()
    beside = up[...] + down[...]
    out = next_field(parts, (c0, c1, c2, c3), field, None, diag, beside, fetch.wait)
    field_out[...] = out
    store_parts(send, out, row_ref[0] % NY)


def step(row_ref, parts, c0, c1, c2, c3, diag, up, down, field, previous, field_out, send):
    out = next_field(parts, (c0, c1, c2, c3), field, previous, diag, up[...] + down[...])
    field_out[...] = out
    store_parts(send, out, row_ref[0] % NY)


def last_step(parts, c0, c1, c2, c3, field, diag, f0, f1, f2, u0, d0, u1, d1, u2, d2, send):
    partial = next_field(parts, (c0, c1, c2, c3), field, f2, diag, None)
    f3 = field[...]
    fields = [f0[...], f1[...], f2[...], f3]
    beside = [u0[...] + d0[...], u1[...] + d1[...], u2[...] + d2[...]]
    lane = lax.broadcasted_iota(jnp.int32, (B, 128), 1)
    table = jnp.zeros((B, 128), F32)
    for p, (i, j) in enumerate(PAIRS):
        if j < STEPS:
            terms = fields[i] * fields[j]
        elif i < STEPS - 1:
            terms = partial * fields[i] - f3 * beside[i] * (1.0 / SCALE)
        else:
            continue
        table = jnp.where(lane == p, jnp.sum(terms, axis=1, keepdims=True), table)
    packed = jnp.concatenate([table, partial, f3], axis=1)
    for k in range(NX * NC):
        send[k] = packed


def add_up(plane_ref, packed, last_out, send):
    count = NX * NC
    inv = 1.0 / SCALE

    def partial(p):
        return packed[p][:, 128 : 128 + W]

    def before(p):
        return packed[p][:, 128 + W :]

    table = packed[0][:, :128]
    for p in range(1, count):
        table = table + packed[p][:, :128]
    square = cross = jnp.zeros((B, W), F32)
    for p in range(count):
        beside = before(p - 1) if p > 0 else 0.0
        if p + 1 < count:
            beside = beside + before(p + 1)
        last = partial(p) - beside * inv
        square = square + last * last
        cross = cross + last * before(p)
    lane = lax.broadcasted_iota(jnp.int32, (B, 128), 1)
    for pair, terms in (((STEPS - 1, STEPS), cross), ((STEPS, STEPS), square)):
        value = jnp.sum(terms, axis=1, keepdims=True)
        table = jnp.where(lane == PAIRS.index(pair), value, table)
    for z in range(NZ):
        send[z] = table
    plane = plane_ref[0] // NY
    above = jnp.where(plane > 0, before(jnp.maximum(plane - 1, 0)), 0.0)
    below = jnp.where(plane + 1 < count, before(jnp.minimum(plane + 1, count - 1)), 0.0)
    last_out[...] = partial(plane) - (above + below) * inv


def finish(tables, f0, f1, f2, f3, f4, solution_out, residual_out):
    total = tables[0]
    for z in range(1, NZ):
        total = total + tables[z]
    gram = {}
    for p, (i, j) in enumerate(PAIRS):
        gram[i, j] = gram[j, i] = total[:, p : p + 1]

    def inner(a, c):
        total = None
        for j, cj in enumerate(c):
            part = None
            for i, ai in enumerate(a):
                term = gram[i, j] if ai is None else ai * gram[i, j]
                part = term if part is None else part + term
            part = part if cj is None else part * cj
            total = part if total is None else total + part
        return total

    def plus(a, c, scale):
        out = []
        for k in range(max(len(a), len(c))):
            if k >= len(c):
                out.append(a[k])
            elif k >= len(a):
                out.append(scale * c[k])
            else:
                out.append(a[k] + scale * c[k])
        return out

    def image(a):
        out = [CENTRE * x for x in a] + [jnp.zeros_like(a[0])]
        for k, x in enumerate(a):
            out[k + 1] = out[k + 1] + SCALE * x
            if k > 0:
                out[k - 1] = out[k - 1] + LINK * x
        return out

    one = jnp.ones((B, 1), F32)
    source = [None]
    found = None
    residual = search = [one]
    rho = gram[0, 0]
    for iteration in range(2):
        image_one = image(search)
        alpha = rho / inner(source, image_one)
        interim = plus(residual, image_one, -alpha)
        image_two = image(interim)
        omega = inner(image_two, interim) / inner(image_two, image_two)
        if found is None:
            found = [alpha * x for x in search]
        else:
            found = plus(found, search, alpha)
        found = plus(found, interim, omega)
        residual = plus(interim, image_two, -omega)
        if iteration == 0:
            rho_next = inner(source, residual)
            beta = (rho_next / rho) * (alpha / omega)
            search = plus(residual, plus(search, image_one, -omega), beta)
            rho = rho_next
    fields = [f[:, :H] for f in (f0, f1, f2, f3, f4)]

    def combine(a):
        out = a[0] * fields[0]
        for k in range(1, len(a)):
            out = out + a[k] * fields[k]
        return out

    solution_out[...] = combine(found)
    residual_out[...] = combine(residual)


def swapped(array, mask):
    return lax.ppermute(array, "y", [(y, y ^ mask) for y in range(NY)])


def even(field):
    return lax.ppermute(field, ("x", "c"), [(i, i ^ 1) for i in range(NX * NC)])


def odd(field):
    pairs = [(i, i + 1) for i in range(1, NX * NC - 1, 2)]
    return lax.ppermute(field, ("x", "c"), pairs + [(j, i) for i, j in pairs])


def on_device(source, coupling, diagonal):
    own = coupling[0]
    row = lax.axis_index(("x", "c", "y")).astype(jnp.int32).reshape(1)
    packed = jnp.concatenate([source[0], jnp.broadcast_to(diagonal, (B, H))], axis=1)
    packed = jnp.broadcast_to(packed[None], (NC * NY, B, 128))
    packed = lax.all_to_all(packed, ("c", "y"), 0, 0, tiled=True)
    by_1, by_3 = swapped(own, 1), swapped(own, 3)
    by_1, packed = lax.optimization_barrier((by_1, packed))
    blocks = [own, by_1, swapped(by_1, 3), by_3]
    shape = jax.ShapeDtypeStruct
    wide = shape((B, W), F32)
    sends = [shape((NZ, 2 * B if low else B, W), BF16) for low in WITH_LOW]
    field, up, diag, send = call(unpack, (wide, wide, wide, sends[0]), row, packed, smem=1)
    fields, beside = [field], []
    for k in range(STEPS - 1):
        down = odd(field)
        if k > 0:
            up = even(field)
        beside += [up, down]
        parts = lax.all_to_all(send, "z", 0, 0, tiled=True)
        outs = (wide, sends[k + 1])
        if k == 0:
            field, send, blocks[0] = call(
                first_step, (*outs, shape((H, NZ * W), BF16)), row, own, parts, *blocks[1:], diag, up, down, field,
                smem=1,
                hbm=1,
                scratch=[pltpu.SemaphoreType.DMA],
            )
        else:
            field, send = call(
                step, outs, row, parts, *blocks, diag, up, down, *fields[::-1][:2], smem=1
            )
        fields.append(field)
    parts = lax.all_to_all(send, "z", 0, 0, tiled=True)
    packed = call(
        last_step,
        shape((NX * NC, B, 128 + 2 * W), F32),
        parts, *blocks, field, diag, *fields[:3], *beside,
    )
    packed = lax.all_to_all(packed, ("x", "c"), 0, 0, tiled=True)
    last, table = call(add_up, (wide, shape((NZ, B, 128), F32)), row, packed, smem=1)
    table = lax.all_to_all(table, "z", 0, 0, tiled=True)
    own_shape = shape((B, H), F32)
    found, residual = call(finish, (own_shape, own_shape), table, *fields, last, keep=False)
    return found[None], residual[None]


def solution(mesh):
    fine = Mesh(mesh.devices.reshape(NX, NC, NZ, NY), ("x", "c", "z", "y"))
    depth, harm = ("x", "c"), ("z", "y")
    return jax.shard_map(
        on_device,
        mesh=fine,
        in_specs=(P(depth, None, harm), P(depth, harm, None), P(depth, harm)),
        out_specs=(P(depth, None, harm), P(depth, None, harm)),
        check_vma=False,
    )
```
